32 devices in a mesh: groups: 2 (over y), expert: 8 (over z, core), section: 2 (over x), tensor: 1.
Axes of the slice: x: 2, y: 2, z: 4, core: 2. Of those that a mesh axis runs over, the one named last changes fastest.
Arguments:
- opening_residual: bfloat16 [2, 2048, 2048], P('section', ('groups', 'expert'), 'tensor'), parts along dimension 1, may hold values from -12 to 12
- incoming_residual: bfloat16 [1, 2048, 2048], P(None, ('groups', 'expert'), 'tensor'), parts along dimension 1, may hold values from -12 to 12
- stored_summaries: bfloat16 [2, 2, 16, 768, 512], P(None, 'section', ('groups', 'expert')), parts along dimension 2, may hold values from -40 to 40
- stored_counts: int32 [3, 16], P(None, ('groups', 'expert')), parts along dimension 1, may hold values from 1 to 768, as said below
- picked_specialists: int32 [2, 2, 2048, 6], P(None, 'section', ('groups', 'expert')), parts along dimension 2, may hold values from 0 to 15, all different within a row; in each aligned block of 128 rows (0 to 127, 128 to 255, ..., all dimensions but the last counted through in order) at most 64 rows name the same one
- chooser_mixing_share: float32 [2, 2, 2048, 6], P(None, 'section', ('groups', 'expert')), parts along dimension 2, may hold values from 0.05 to 0.4
- mixing_scale_factor: float32 [2, 2048], P('section'), may hold values from 0.25 to 1.75
- asking_projection: bfloat16 [2, 2048, 1024], P('section', None, 'tensor'), may hold values from -0.125 to 0.125
- summary_lookup_factor: bfloat16 [2, 8, 128, 512], P('section', 'tensor'), may hold values from -0.5 to 0.5
- summary_content_factor: bfloat16 [2, 8, 512, 128], P('section', 'tensor'), may hold values from -0.25 to 0.25
- merging_projection: bfloat16 [2, 1024, 2048], P('section', 'tensor'), may hold values from -0.1875 to 0.1875
- compress_projection: bfloat16 [2, 2048, 512], P('section', None, 'tensor'), may hold values from -0.125 to 0.125
- summary_scale_factor: float32 [2, 512], P('section'), may hold values from 0.25 to 1.75
- specialist_scale_factor: float32 [2, 2048], P('section', 'tensor'), may hold values from 0.25 to 1.75
- specialist_switch_factor: bfloat16 [2, 16, 2048, 704], P('section', 'expert', None, 'tensor'), may hold values from -0.125 to 0.125
- specialist_widen_factor: bfloat16 [2, 16, 2048, 704], P('section', 'expert', None, 'tensor'), may hold values from -0.125 to 0.125
- specialist_contract_factor: bfloat16 [2, 16, 704, 2048], P('section', 'expert', 'tensor'), may hold values from -0.21875 to 0.21875
Outputs:
- results: bfloat16 [2, 2, 2048, 2048], P(None, 'section', ('groups', 'expert'), 'tensor'), parts along dimension 2
The draws below stay inside these ranges and needn't reach their ends.
There are 2 independent parts, one for each index of `groups`. The reference program is written for one: setup_inputs(seed, part) draws one part's arguments, and reference() takes and returns one part's arrays. A program takes and returns all parts, laid end to end along the dimension named above; an argument that names none is the same for every part. Nothing has to cross between parts.
Inputs may be any that keep to these rules, and one draw needn't show every extreme that they name: `picked_specialists`: in each aligned block of 128 rows (one sequence) no expert is chosen by more than 64 rows, a bound that some block reaches; each row names 6 different experts. `stored_counts`: in every microbatch some sequence has exactly 768 cached tokens.
All inputs are finite; a program needn't handle non-finite values.
Results may differ from the reference program's by a relative error of at most 0.04.
Values may be sent and summed in bfloat16 or wider, within the bound.
A program may use at most 128 MiB of HBM per device.

```python
import math
import jax
import jax.numpy as jnp
import numpy as np
from jax import lax

D = 2048
HD = 128
LAT = 512
TOP = 6
HEADS = 8
FFE = 704
EXPERTS = 16
TICKS = 2
TOK_DEV = 128
CTX = 768
SECTIONS = 2
SEQS = 8
ROWS = 1024
MICRO = 3
CAP = 64
N_TENSOR = 1


def activation_draw(key, array_shape):
    key_values, key_scale, key_column = jax.random.split(key, 3)
    row_scale = jnp.exp(jax.random.uniform(key_scale, array_shape[:-1] + (1,), jnp.float32, math.log(0.3), math.log(1.5)))
    width = array_shape[-1]
    ramp = jnp.arange(width, dtype=jnp.float32) / (width - 1)
    jitter = jnp.exp(jax.random.uniform(key_column, (width,), jnp.float32, -0.15, 0.15))
    column_scale = jnp.exp(math.log(0.5) + ramp * math.log(4.0)) * jitter
    values = jnp.clip(jax.random.normal(key_values, array_shape, jnp.float32), -3.5, 3.5)
    return jnp.clip(values * row_scale * column_scale, -12.0, 12.0)


def draw_opening_residual(key, part):
    return activation_draw(jax.random.fold_in(key, 11), (SECTIONS, ROWS, D)).astype(jnp.bfloat16)


def draw_incoming_residual(key, part):
    return activation_draw(jax.random.fold_in(key, 23), (TICKS - 1, ROWS, D)).astype(jnp.bfloat16)


def draw_stored_summaries(key, part):
    key_values = jax.random.fold_in(jax.random.fold_in(key, 37), 0)
    array_shape = (TICKS, SECTIONS, SEQS, CTX, LAT)
    values = jnp.clip(jax.random.normal(key_values, array_shape, jnp.float32), -4.0, 4.0)
    return values.astype(jnp.bfloat16)


def draw_stored_counts(key, part):
    key_values, key_full = jax.random.split(jax.random.fold_in(key, 41))
    values = jax.random.randint(key_values, (MICRO, SEQS), 1, CTX + 1).astype(jnp.int32)
    full_seq = jax.random.randint(key_full, (MICRO, 1), 0, SEQS).astype(jnp.int32)
    seq_index = jnp.arange(SEQS, dtype=jnp.int32)[None, :]
    return jnp.where(seq_index == full_seq, CTX, values).astype(jnp.int32)


def block_scale(own_key, extent, pieces, low, largest):
    loudness = 1.0
    for dim, parts in pieces:
        steps = jax.random.uniform(jax.random.fold_in(jax.random.fold_in(own_key, 6), dim), (parts,), jnp.float32, low / len(pieces), largest / len(pieces))
        loudness = loudness * jnp.repeat(jnp.exp(steps), extent[dim] // parts).reshape((-1,) + (1,) * (len(extent) - 1 - dim))
    return loudness


def routed_block(stream_key, own, number, rows, number_of, top, limit, slope):
    ranking = jax.random.permutation(stream_key, number_of)
    heavy_load, ordinary = shares(number_of, rows * top, limit, slope, True), shares(number_of, rows * top, limit, slope, False)
    places = jnp.arange(number_of)

    def named(sizes, offset_by):
        used = int((sizes > 0).sum())
        fixed = max(1, used // 4)
        moved = fixed + (places - fixed + offset_by * (used - fixed)) % max(1, number_of - fixed)
        return jnp.zeros((number_of,), jnp.int32).at[ranking[jnp.where(places < fixed, places, moved)]].set(jnp.asarray(sizes, jnp.int32))

    sizes = jnp.where(number % 4 == 0, named(heavy_load, number // 4), named(ordinary, number - number // 4 - 1))
    mixed = jax.random.permutation(jax.random.fold_in(own, 3), number_of)
    giver, receiver = mixed[0:number_of // 2 * 2:2], mixed[1:number_of // 2 * 2:2]
    margin = jnp.minimum(sizes[giver] - 1, limit - sizes[receiver]) // 2
    margin = jnp.where((giver == ranking[0]) | (receiver == ranking[0]) | (sizes[receiver] == 0), 0, jnp.maximum(margin, 0))
    moved = jax.random.randint(jax.random.fold_in(own, 4), (number_of // 2,), 0, 1 << 20) % (margin + 1)
    sizes = sizes.at[giver].add(-moved).at[receiver].add(moved)
    members = jnp.searchsorted(jnp.cumsum(sizes), jnp.arange(rows * top), side="right").astype(jnp.int32)
    listing = members.reshape(top, rows).T
    listing = listing[jax.random.permutation(jax.random.fold_in(own, 1), rows)]
    offset_by = jax.random.randint(jax.random.fold_in(own, 2), (rows, 1), 0, top)
    return jnp.take_along_axis(listing, (jnp.arange(top)[None, :] + offset_by) % top, axis=1)


def shares(amount, total, reach, lean, full):
    weights = [(1 << 20) // math.isqrt(standing ** lean) + 1 for standing in range(1, amount + 1)]
    largest = reach if full else min(reach, max(-(-total // amount), total * weights[0] // sum(weights)))
    least = 1 if total - largest >= amount - 1 else 0
    holding, surplus = [largest] + [least] * (amount - 1), total - largest - least * (amount - 1)
    while surplus > 0:
        candidates = [i for i in range(1, amount) if holding[i] < largest] or [i for i in range(1, amount) if holding[i] < reach]
        pool, left = sum([weights[i] for i in candidates]), surplus
        for i in candidates:
            addition = min(reach - holding[i], max(1, left * weights[i] // pool), surplus)
            holding[i] = holding[i] + addition
            surplus = surplus - addition
    return np.array(holding)


def bell_draw(stream_key, extent, scale, reach, shards=(), kind=jnp.bfloat16):
    result = jax.random.normal(stream_key, extent, jnp.float32) * scale
    if len(shards) > 0:
        result = block_scale(stream_key, extent, shards, -0.22, 0.18) * result
    return jnp.clip(result, min=-reach, max=reach).astype(kind)


def setup_inputs(seed: int = 0, part: int = 0) -> dict:
    seeds = jax.random.split(jax.random.key(seed), 18)
    part_keys = jax.random.split(jax.random.fold_in(seeds[17], part), 18)
    opening_residual = draw_opening_residual(jax.random.fold_in(jax.random.fold_in(seeds[17], part), 71), part)
    incoming_residual = draw_incoming_residual(jax.random.fold_in(jax.random.fold_in(seeds[17], part), 71), part)
    stored_summaries = draw_stored_summaries(jax.random.fold_in(jax.random.fold_in(seeds[17], part), 71), part)
    stored_counts = draw_stored_counts(jax.random.fold_in(jax.random.fold_in(seeds[17], part), 71), part)
    picked_specialists_keys = jax.random.split(jax.random.fold_in(part_keys[4], 1), TICKS * SECTIONS * ROWS // TOK_DEV)
    picked_specialists_turns = jax.random.permutation(jax.random.fold_in(part_keys[4], 3), TICKS * SECTIONS * ROWS // TOK_DEV)
    picked_specialists = jax.vmap(lambda own, number: routed_block(jax.random.fold_in(part_keys[4], 2), own, number, TOK_DEV, EXPERTS, TOP, CAP, 2))(picked_specialists_keys, picked_specialists_turns).reshape((TICKS, SECTIONS, ROWS, TOP))
    chooser_mixing_share = jnp.clip(0.05 + 0.35 * jax.random.uniform(part_keys[5], (TICKS, SECTIONS, ROWS, TOP), jnp.float32) ** block_scale(part_keys[5], (TICKS, SECTIONS, ROWS, TOP), ((1, 2), (2, 8)), -0.2, 0.2), 0.05, 0.4)
    mixing_scale_factor = jnp.clip(1.0 + 0.15 * jax.random.normal(seeds[6], (SECTIONS, D), jnp.float32), 0.25, 1.75)
    asking_projection = bell_draw(seeds[7], (SECTIONS, D, HEADS * HD), D ** -0.5, 0.125, ((0, 2),))
    summary_lookup_factor = bell_draw(seeds[8], (SECTIONS, HEADS, HD, LAT), HD ** -0.5, 0.5, ((0, 2),))
    summary_content_factor = bell_draw(seeds[9], (SECTIONS, HEADS, LAT, HD), LAT ** -0.5, 0.25, ((0, 2),))
    merging_projection = bell_draw(seeds[10], (SECTIONS, HEADS * HD, D), (HEADS * HD) ** -0.5, 0.1875, ((0, 2),))
    compress_projection = bell_draw(seeds[11], (SECTIONS, D, LAT), D ** -0.5, 0.125, ((0, 2),))
    summary_scale_factor = jnp.clip(1.0 + 0.15 * jax.random.normal(seeds[12], (SECTIONS, LAT), jnp.float32), 0.25, 1.75)
    specialist_scale_factor = jnp.clip(1.0 + 0.15 * jax.random.normal(seeds[13], (SECTIONS, D), jnp.float32), 0.25, 1.75)
    specialist_switch_factor = bell_draw(seeds[14], (SECTIONS, EXPERTS, D, FFE), D ** -0.5, 0.125, ((0, 2), (1, 8)))
    specialist_widen_factor = bell_draw(seeds[15], (SECTIONS, EXPERTS, D, FFE), D ** -0.5, 0.125, ((0, 2), (1, 8)))
    specialist_contract_factor = bell_draw(seeds[16], (SECTIONS, EXPERTS, FFE, D), FFE ** -0.5, 0.21875, ((0, 2), (1, 8)))
    return {"opening_residual": opening_residual, "incoming_residual": incoming_residual, "stored_summaries": stored_summaries, "stored_counts": stored_counts, "picked_specialists": picked_specialists, "chooser_mixing_share": chooser_mixing_share, "mixing_scale_factor": mixing_scale_factor, "asking_projection": asking_projection, "summary_lookup_factor": summary_lookup_factor, "summary_content_factor": summary_content_factor, "merging_projection": merging_projection, "compress_projection": compress_projection, "summary_scale_factor": summary_scale_factor, "specialist_scale_factor": specialist_scale_factor, "specialist_switch_factor": specialist_switch_factor, "specialist_widen_factor": specialist_widen_factor, "specialist_contract_factor": specialist_contract_factor}


epsilon = 1e-06

def row_norm(values, gain_row):
    return values * lax.rsqrt(lax.optimization_barrier(jnp.mean(values * values, axis=-1, keepdims=True)) + epsilon) * gain_row

def attend(q_lat, cache_rows, new_rows, length):
    key_rows = jnp.concatenate([cache_rows, new_rows], axis=0)
    scores = jnp.einsum('thl,kl->thk', q_lat.astype(jnp.float32), key_rows.astype(jnp.float32)) * HD ** (-0.5)
    position = jnp.arange(CTX + TOK_DEV, dtype=jnp.int32)[None, :]
    query_pos = jnp.arange(TOK_DEV, dtype=jnp.int32)[:, None]
    visible = jnp.where(position < CTX, position < length, position - CTX <= query_pos)
    scores = jnp.where(visible[:, None, :], scores, -jnp.inf)
    row_max = lax.optimization_barrier(jnp.max(scores, axis=-1, keepdims=True))
    expd = jnp.where(visible[:, None, :], jnp.exp(scores - row_max), 0.0)
    attention = (expd / lax.optimization_barrier(jnp.sum(expd, axis=-1, keepdims=True))).astype(jnp.bfloat16)
    return jnp.einsum('thk,kl->thl', attention.astype(jnp.float32), key_rows.astype(jnp.float32)).astype(jnp.bfloat16)

def run_layer(inner_response, cache_now, lengths_now, route, gates, segment_ordinal, mixing_scale_factor, asking_projection, summary_lookup_factor, summary_content_factor, merging_projection, compress_projection, summary_scale_factor, specialist_scale_factor, specialist_switch_factor, specialist_widen_factor, specialist_contract_factor):
    start_rows = inner_response.astype(jnp.float32)
    normed = row_norm(start_rows, mixing_scale_factor[segment_ordinal]).astype(jnp.bfloat16)
    queries = jnp.dot(normed, asking_projection[segment_ordinal], preferred_element_type=jnp.float32).astype(jnp.bfloat16)
    queries = queries.reshape(ROWS, HEADS, HD)
    q_lat = jnp.einsum('rnd,ndl->rnl', queries.astype(jnp.float32), summary_lookup_factor[segment_ordinal].astype(jnp.float32)).astype(jnp.bfloat16)
    latent_raw = jnp.dot(normed, compress_projection[segment_ordinal], preferred_element_type=jnp.float32)
    new_latent = row_norm(latent_raw, summary_scale_factor[segment_ordinal]).astype(jnp.bfloat16)
    o_lat = lax.map(lambda packed: attend(packed[0], packed[1], packed[2], packed[3]), (q_lat.reshape(SEQS, TOK_DEV, HEADS, LAT), cache_now, new_latent.reshape(SEQS, TOK_DEV, LAT), lengths_now))
    o_lat = o_lat.reshape(ROWS, HEADS, LAT)
    heads_out = jnp.einsum('rnl,nld->rnd', o_lat.astype(jnp.float32), summary_content_factor[segment_ordinal].astype(jnp.float32)).astype(jnp.bfloat16)
    heads_out = heads_out.reshape(ROWS, HEADS * HD)
    residual = start_rows + jnp.dot(heads_out, merging_projection[segment_ordinal], preferred_element_type=jnp.float32)
    moe_input = row_norm(residual, specialist_scale_factor[segment_ordinal]).astype(jnp.bfloat16)
    choices = route.reshape(SEQS, TOK_DEV * TOP).astype(jnp.int32)
    onehot = (choices[:, :, None] == jnp.arange(EXPERTS, dtype=jnp.int32)[None, None, :]).astype(jnp.int32)
    earlier = jnp.cumsum(onehot, axis=1) - onehot
    slot_index = lax.optimization_barrier(jnp.sum(earlier * onehot, axis=2))
    block_index = jnp.arange(SEQS, dtype=jnp.int32)[:, None]
    target = (choices * (SEQS * CAP) + block_index * CAP + slot_index).reshape(-1).astype(jnp.int32)
    source = jnp.repeat(jnp.arange(ROWS, dtype=jnp.int32), TOP)
    buffer = jnp.zeros((EXPERTS * SEQS * CAP, D), jnp.bfloat16).at[target].set(moe_input[source])
    buffer = buffer.reshape(EXPERTS, SEQS * CAP, D)

    def one_expert(packed):
        rows_in, gate_mat, up_mat, down_mat = packed
        gate_values = jnp.dot(rows_in, gate_mat, preferred_element_type=jnp.float32)
        up_values = jnp.dot(rows_in, up_mat, preferred_element_type=jnp.float32)
        hidden = (jax.nn.silu(gate_values) * up_values).astype(jnp.bfloat16)
        hidden_parts = hidden.reshape(SEQS * CAP, N_TENSOR, FFE // N_TENSOR).astype(jnp.float32)
        down_parts = down_mat.reshape(N_TENSOR, FFE // N_TENSOR, D).astype(jnp.float32)
        partial_value = jnp.einsum('mpf,pfd->pmd', hidden_parts, down_parts).astype(jnp.bfloat16)
        return lax.optimization_barrier(jnp.sum(partial_value.astype(jnp.float32), axis=0)).astype(jnp.bfloat16)
    expert_out = lax.map(one_expert, (buffer, specialist_switch_factor[segment_ordinal], specialist_widen_factor[segment_ordinal], specialist_contract_factor[segment_ordinal]))
    picked = expert_out.reshape(EXPERTS * SEQS * CAP, D)[target].astype(jnp.float32).reshape(ROWS, TOP, D)
    routed = lax.optimization_barrier(jnp.sum(picked * gates[:, :, None], axis=1))
    return (residual + routed).astype(jnp.bfloat16)

def reference(opening_residual, incoming_residual, stored_summaries, stored_counts, picked_specialists, chooser_mixing_share, mixing_scale_factor, asking_projection, summary_lookup_factor, summary_content_factor, merging_projection, compress_projection, summary_scale_factor, specialist_scale_factor, specialist_switch_factor, specialist_widen_factor, specialist_contract_factor):
    outputs = []
    previous = []
    for step_index in range(TICKS):
        current_row = []
        for segment_ordinal in range(SECTIONS):
            if step_index == 0:
                inner_response = opening_residual[segment_ordinal]
            elif segment_ordinal == 0:
                inner_response = incoming_residual[step_index - 1]
            else:
                inner_response = previous[segment_ordinal - 1]
            micro_index = step_index - segment_ordinal + SECTIONS - 1
            result_rows = run_layer(inner_response, stored_summaries[step_index, segment_ordinal], stored_counts[micro_index], picked_specialists[step_index, segment_ordinal], chooser_mixing_share[step_index, segment_ordinal], segment_ordinal, mixing_scale_factor, asking_projection, summary_lookup_factor, summary_content_factor, merging_projection, compress_projection, summary_scale_factor, specialist_scale_factor, specialist_switch_factor, specialist_widen_factor, specialist_contract_factor)
            current_row.append(result_rows)
        previous = current_row
        outputs.append(jnp.stack(current_row))
    return jnp.stack(outputs)
```

```python
import jax
import jax.numpy as jnp
from jax import lax
from jax.sharding import PartitionSpec as P

CAP = 64
RETURN_CHUNKS = 2


epsilon = 1e-06


def shifted(value, axis, steps):
    count = lax.axis_size(axis)
    initial, last = (max(0, -steps), min(count, count - steps))
    return lax.ppermute(value, axis, [(source, source + steps) for source in range(initial, last)])


def row_norm(values, gain_row):
    return (
        values * lax.rsqrt(jnp.mean(values * values, axis=-1, keepdims=True) + epsilon) * gain_row
    )


def attend(q_lat, cache_rows, new_rows, length, score_scale):
    piece_list = q_lat.shape[0]
    context = cache_rows.shape[0]
    key_rows = jnp.concatenate([cache_rows, new_rows], axis=0)
    scores = (
        jnp.einsum("thl,kl->thk", q_lat, key_rows, preferred_element_type=jnp.float32) * score_scale
    )
    position = lax.broadcasted_iota(jnp.int32, (piece_list, context + piece_list), 1)
    query_pos = lax.broadcasted_iota(jnp.int32, (piece_list, context + piece_list), 0)
    visible = jnp.where(position < context, position < length, position - context <= query_pos)
    scores = jnp.where(visible[:, None, :], scores, -jnp.inf)
    row_max = jnp.max(scores, axis=-1, keepdims=True)
    expd = jnp.where(visible[:, None, :], jnp.exp(scores - row_max), 0.0)
    attention = (expd / jnp.sum(expd, axis=-1, keepdims=True)).astype(jnp.bfloat16)
    return jnp.einsum(
        "thk,kl->thl", attention, key_rows, preferred_element_type=jnp.float32
    ).astype(jnp.bfloat16)


def shards(
    opening_residual,
    incoming_residual,
    stored_summaries,
    stored_counts,
    picked_specialists,
    chooser_mixing_share,
    mixing_scale_factor,
    asking_projection,
    summary_lookup_factor,
    summary_content_factor,
    merging_projection,
    compress_projection,
    summary_scale_factor,
    specialist_scale_factor,
    specialist_switch_factor,
    specialist_widen_factor,
    specialist_contract_factor,
):
    segment_ordinal = lax.axis_index("section")
    section_count = lax.axis_size("section")
    sources = lax.axis_size("expert")
    tick_count = stored_summaries.shape[0]
    piece_list = opening_residual.shape[1]
    inner_feature_midcount = opening_residual.shape[2]
    full_width = mixing_scale_factor.shape[1]
    local_heads = summary_lookup_factor.shape[1]
    head_size = summary_lookup_factor.shape[2]
    top_count = picked_specialists.shape[3]
    expert_local = specialist_switch_factor.shape[1]
    score_scale = head_size ** (-0.5)
    expert_ids = lax.broadcasted_iota(jnp.int32, (1, 1, 1, expert_local * sources), 3)
    shares_dense = jnp.sum(
        jnp.where(
            picked_specialists[:, 0][..., None] == expert_ids,
            chooser_mixing_share[:, 0][..., None],
            0.0,
        ),
        axis=2,
    )
    shares_all = lax.all_gather(
        jnp.swapaxes(shares_dense, 1, 2), "expert", axis=1, tiled=False
    )
    mine = lax.dynamic_slice_in_dim(
        shares_all, lax.axis_index("expert") * expert_local, expert_local, axis=2
    )
    chosen = mine > 0.0
    earlier_or_same = (
        lax.broadcasted_iota(jnp.int32, (piece_list, piece_list), 0)
        <= lax.broadcasted_iota(jnp.int32, (piece_list, piece_list), 1)
    ).astype(jnp.bfloat16)
    rank = jnp.einsum(
        "tjer,rq->tjeq",
        chosen.astype(jnp.bfloat16),
        earlier_or_same,
        preferred_element_type=jnp.float32,
    ).astype(jnp.int32)
    slots = lax.broadcasted_iota(jnp.int32, (1, 1, 1, CAP, 1), 3) + 1
    at_slot = (rank[..., None, :] == slots) & chosen[..., None, :]
    placed = at_slot.astype(jnp.bfloat16)
    slot_share = jnp.sum(jnp.where(at_slot, mine[..., None, :], 0.0), axis=-1)
    outputs = []
    present_carry = opening_residual[0]
    section_out = present_carry
    for step_index in range(tick_count):
        if step_index > 0:
            handed = shifted(section_out, "section", 1)
            present_carry = jnp.where(
                segment_ordinal == 0, incoming_residual[step_index - 1], handed
            )
        micro_index = step_index - segment_ordinal + section_count - 1
        length = lax.dynamic_index_in_dim(stored_counts[:, 0], micro_index, 0, keepdims=False)
        full_rows = lax.all_gather(present_carry, "tensor", axis=1, tiled=True)
        normed = row_norm(full_rows.astype(jnp.float32), mixing_scale_factor[0]).astype(
            jnp.bfloat16
        )
        queries = jnp.dot(normed, asking_projection[0], preferred_element_type=jnp.float32).astype(
            jnp.bfloat16
        )
        queries = queries.reshape(piece_list, local_heads, head_size)
        q_lat = jnp.einsum(
            "thd,hdl->thl", queries, summary_lookup_factor[0], preferred_element_type=jnp.float32
        ).astype(jnp.bfloat16)
        latent_part = jnp.dot(normed, compress_projection[0], preferred_element_type=jnp.float32)
        latent_raw = lax.all_gather(
            latent_part.astype(jnp.bfloat16), "tensor", axis=1, tiled=True
        ).astype(latent_part.dtype)
        new_latent = row_norm(latent_raw, summary_scale_factor[0]).astype(jnp.bfloat16)
        o_lat = attend(q_lat, stored_summaries[step_index, 0, 0], new_latent, length, score_scale)
        heads_out = jnp.einsum(
            "thl,hld->thd", o_lat, summary_content_factor[0], preferred_element_type=jnp.float32
        ).astype(jnp.bfloat16)
        heads_out = heads_out.reshape(piece_list, local_heads * head_size)
        head_terms = jnp.dot(heads_out, merging_projection[0], preferred_element_type=jnp.float32)
        residual = present_carry.astype(jnp.float32) + lax.psum_scatter(
            head_terms.astype(jnp.bfloat16), "tensor", scatter_dimension=1, tiled=True
        ).astype(jnp.float32)
        squares = lax.psum(jnp.sum(residual * residual, axis=1), "tensor")
        moe_input = (
            residual
            * lax.rsqrt(squares / full_width + epsilon)[:, None]
            * specialist_scale_factor[0]
        ).astype(jnp.bfloat16)
        whole_rows = lax.all_gather(moe_input, "tensor", axis=1, tiled=True)
        place = placed[step_index]
        share = slot_share[step_index]
        all_rows = lax.all_gather(whole_rows, "expert", axis=0, tiled=True)
        all_rows = all_rows.reshape(sources, piece_list, full_width)
        hidden_list = []
        for e in range(expert_local):
            rows_in = jnp.einsum(
                "jsr,jrd->jsd", place[:, e], all_rows, preferred_element_type=jnp.float32
            ).astype(jnp.bfloat16)
            rows_in = rows_in.reshape(sources * CAP, full_width)
            gate_values = jnp.dot(
                rows_in, specialist_switch_factor[0, e], preferred_element_type=jnp.float32
            )
            up_values = jnp.dot(
                rows_in, specialist_widen_factor[0, e], preferred_element_type=jnp.float32
            )
            hidden_list.append(
                (jax.nn.silu(gate_values) * up_values * share[:, e].reshape(-1, 1)).astype(
                    jnp.bfloat16
                )
            )
        chunk = full_width // RETURN_CHUNKS
        routed_list = []
        for c in range(RETURN_CHUNKS):
            total = None
            for e in range(expert_local):
                down = jnp.dot(
                    hidden_list[e],
                    specialist_contract_factor[0, e][:, c * chunk : (c + 1) * chunk],
                    preferred_element_type=jnp.float32,
                ).astype(jnp.bfloat16)
                term = jnp.einsum(
                    "jsr,jsd->jrd",
                    place[:, e],
                    down.reshape(sources, CAP, chunk),
                    preferred_element_type=jnp.float32,
                )
                total = term if total is None else total + term
            total = total.astype(jnp.bfloat16).reshape(sources * piece_list, chunk)
            routed_list.append(
                lax.psum_scatter(total, "expert", scatter_dimension=0, tiled=True)
            )
        routed = jnp.concatenate(routed_list, axis=1)
        routed = lax.psum_scatter(routed, "tensor", scatter_dimension=1, tiled=True).astype(
            jnp.float32
        )
        section_out = (residual + routed).astype(jnp.bfloat16)
        outputs.append(section_out)
    return jnp.stack(outputs)[:, None]


def solution(mesh):
    in_specs = (
        P("section", ("groups", "expert"), "tensor"),
        P(None, ("groups", "expert"), "tensor"),
        P(None, "section", ("groups", "expert"), None, None),
        P(None, ("groups", "expert")),
        P(None, "section", ("groups", "expert"), None),
        P(None, "section", ("groups", "expert"), None),
        P("section", None),
        P("section", None, "tensor"),
        P("section", "tensor", None, None),
        P("section", "tensor", None, None),
        P("section", "tensor", None),
        P("section", None, "tensor"),
        P("section", None),
        P("section", "tensor"),
        P("section", "expert", None, "tensor"),
        P("section", "expert", None, "tensor"),
        P("section", "expert", "tensor", None),
    )
    out_specs = P(None, "section", ("groups", "expert"), "tensor")
    return jax.shard_map(shards, mesh=mesh, in_specs=in_specs, out_specs=out_specs, check_vma=False)
```

```python
import jax
import jax.numpy as jnp
from jax import lax
from jax.experimental import pallas as pl
from jax.experimental.pallas import tpu as pltpu
from jax.sharding import PartitionSpec as P

CAP = 64
RETURN_CHUNKS = 1


epsilon = 1e-06


MESH = pl.DeviceIdType.MESH
PIECES = 2


def place_on_line():
    count = lax.axis_size("expert")
    pair = 2 if count % 2 == 0 else 1
    mine = lax.axis_index("expert")
    return count // pair, pair, mine, mine // pair, lax.rem(mine, pair)


def greet(chips, pair, mine, spot, side):
    barrier = pltpu.get_barrier_semaphore()

    def hello(other):
        pl.semaphore_signal(barrier, inc=1, device_id={"expert": other}, device_id_type=MESH)

    @pl.when(spot > 0)
    def _():
        hello(mine - pair)

    @pl.when(spot < chips - 1)
    def _():
        hello(mine + pair)

    if pair == 2:
        hello(mine + 1 - 2 * side)
    inner = (spot > 0) & (spot < chips - 1)

    @pl.when(inner)
    def _():
        pl.semaphore_wait(barrier, pair + 1)

    @pl.when(jnp.logical_not(inner))
    def _():
        pl.semaphore_wait(barrier, pair)


def remote(src, dst, send, recv, other):
    return pltpu.make_async_remote_copy(
        src_ref=src,
        dst_ref=dst,
        send_sem=send,
        recv_sem=recv,
        device_id={"expert": other},
        device_id_type=MESH,
    )


def spread_kernel(own_ref, all_ref, own_sem, line_send, line_recv, side_send, side_recv):
    chips, pair, mine, spot, side = place_on_line()
    step = own_ref.shape[0] // PIECES
    sibling = mine + 1 - 2 * side

    def rows(block, core, piece):
        return all_ref.at[block, core, pl.ds(piece * step, step)]

    def line_copy(block, piece, way):
        source = own_ref.at[pl.ds(piece * step, step)] if block is None else rows(block, side, piece)
        where = spot if block is None else block
        direction = 0 if way > 0 else 1
        return remote(
            source,
            rows(where, side, piece),
            line_send.at[direction, where, piece],
            line_recv.at[where, piece],
            mine + way * pair,
        )

    def side_copy(block, piece):
        source = own_ref.at[pl.ds(piece * step, step)] if block is None else rows(block, side, piece)
        where = spot if block is None else block
        return remote(
            source,
            rows(where, side, piece),
            side_send.at[where, piece],
            side_recv.at[where, piece],
            sibling,
        )

    def onward(block, piece, way, act):
        @pl.when((spot < chips - 1) if way > 0 else (spot > 0))
        def _():
            act(line_copy(block, piece, way))

    greet(chips, pair, mine, spot, side)
    for piece in range(PIECES):
        for way in (1, -1):
            onward(None, piece, way, lambda copy: copy.start())
    for piece in range(PIECES):
        if pair == 2:
            side_copy(None, piece).start()
    keep = pltpu.make_async_copy(own_ref, all_ref.at[spot, side], own_sem)
    keep.start()
    for far in range(1, chips):
        for piece in range(PIECES):
            for way in (1, -1):
                block = spot - way * far

                @pl.when((block >= 0) if way > 0 else (block < chips))
                def _():
                    line_copy(block, piece, way).wait_recv()
                    onward(block, piece, way, lambda copy: copy.start())
                    if pair == 2:
                        side_copy(block, piece).start()

    keep.wait()
    for piece in range(PIECES):
        for way in (1, -1):
            onward(None, piece, way, lambda copy: copy.wait_send())
        if pair == 2:
            side_copy(None, piece).wait()
    for far in range(1, chips):
        for piece in range(PIECES):
            for way in (1, -1):
                block = spot - way * far

                @pl.when((block >= 0) if way > 0 else (block < chips))
                def _():
                    onward(block, piece, way, lambda copy: copy.wait_send())
                    if pair == 2:
                        side_copy(block, piece).wait()


def spread(own):
    count = lax.axis_size("expert")
    pair = 2 if count % 2 == 0 else 1
    chips = count // pair
    result = pl.pallas_call(
        spread_kernel,
        out_shape=jax.ShapeDtypeStruct((chips, pair) + own.shape, own.dtype),
        in_specs=[pl.BlockSpec(memory_space=pltpu.VMEM)],
        out_specs=pl.BlockSpec(memory_space=pltpu.VMEM),
        scratch_shapes=[
            pltpu.SemaphoreType.DMA,
            pltpu.SemaphoreType.DMA((2, chips, PIECES)),
            pltpu.SemaphoreType.DMA((chips, PIECES)),
            pltpu.SemaphoreType.DMA((chips, PIECES)),
            pltpu.SemaphoreType.DMA((chips, PIECES)),
        ],
        compiler_params=pltpu.CompilerParams(collective_id=0, has_side_effects=True),
    )(own)
    return result.reshape((count,) + own.shape)


def gather_sum_kernel(
    part_ref, sum_ref, side_in, total, line_in, side_send, side_recv, line_send, line_recv
):
    chips, pair, mine, spot, side = place_on_line()
    height = part_ref.shape[2]
    step = height // PIECES
    sibling = mine + 1 - 2 * side

    def span(piece):
        return pl.ds(piece * step, step)

    def side_copy(block, piece):
        return remote(
            part_ref.at[block, 1 - side, span(piece)],
            side_in.at[block, span(piece)],
            side_send.at[block, piece],
            side_recv.at[block, piece],
            sibling,
        )

    def line_copy(block, piece, way):
        direction = 0 if way > 0 else 1
        return remote(
            total.at[block, span(piece)],
            line_in.at[direction, block, span(piece)],
            line_send.at[block, piece],
            line_recv.at[direction, block, piece],
            mine + way * pair,
        )

    def wide(value):
        return value.astype(jnp.float32)

    def chip_sum(block, piece):
        value = wide(part_ref[block, side, span(piece)])
        if pair == 2:
            side_copy(block, piece).wait_recv()
            value = value + wide(side_in[block, span(piece)])
        return value

    greet(chips, pair, mine, spot, side)
    if pair == 2:
        for far in range(chips - 1, -1, -1):
            for piece in range(PIECES):
                for way in (1, -1) if far else (1,):
                    block = spot + way * far

                    @pl.when((block >= 0) & (block < chips))
                    def _():
                        side_copy(block, piece).start()

    for far in range(chips - 1, 0, -1):
        for piece in range(PIECES):
            for way in (1, -1):
                block = spot + way * far

                @pl.when((block >= 0) & (block < chips))
                def _():
                    value = chip_sum(block, piece)
                    total[block, span(piece)] = value.astype(total.dtype)
                    if far < chips - 1:

                        @pl.when((spot > 0) if way > 0 else (spot < chips - 1))
                        def _():
                            direction = 0 if way > 0 else 1
                            line_copy(block, piece, way).wait_recv()
                            total[block, span(piece)] = (
                                wide(total[block, span(piece)])
                                + wide(line_in[direction, block, span(piece)])
                            ).astype(total.dtype)

                    line_copy(block, piece, way).start()

    for piece in range(PIECES):
        total[spot, span(piece)] = chip_sum(spot, piece).astype(total.dtype)
        for way in (1, -1):

            @pl.when((spot > 0) if way > 0 else (spot < chips - 1))
            def _():
                direction = 0 if way > 0 else 1
                line_copy(spot, piece, way).wait_recv()
                total[spot, span(piece)] = (
                    wide(total[spot, span(piece)]) + wide(line_in[direction, spot, span(piece)])
                ).astype(total.dtype)

        sum_ref[span(piece)] = total[spot, span(piece)]
    for far in range(chips - 1, -1, -1):
        for piece in range(PIECES):
            for way in (1, -1) if far else (1,):
                block = spot + way * far

                @pl.when((block >= 0) & (block < chips))
                def _():
                    if far:
                        line_copy(block, piece, way).wait_send()
                    if pair == 2:
                        side_copy(block, piece).wait_send()


def gather_sum(parts):
    count, height, width = parts.shape
    pair = 2 if count % 2 == 0 else 1
    chips = count // pair
    return pl.pallas_call(
        gather_sum_kernel,
        out_shape=jax.ShapeDtypeStruct((height, width), parts.dtype),
        in_specs=[pl.BlockSpec(memory_space=pltpu.VMEM)],
        out_specs=pl.BlockSpec(memory_space=pltpu.VMEM),
        scratch_shapes=[
            pltpu.VMEM((chips, height, width), parts.dtype),
            pltpu.VMEM((chips, height, width), parts.dtype),
            pltpu.VMEM((2, chips, height, width), parts.dtype),
            pltpu.SemaphoreType.DMA((chips, PIECES)),
            pltpu.SemaphoreType.DMA((chips, PIECES)),
            pltpu.SemaphoreType.DMA((chips, PIECES)),
            pltpu.SemaphoreType.DMA((2, chips, PIECES)),
        ],
        compiler_params=pltpu.CompilerParams(collective_id=1, has_side_effects=True),
    )(parts.reshape(chips, pair, height, width))


def shifted(value, axis, steps):
    count = lax.axis_size(axis)
    initial, last = (max(0, -steps), min(count, count - steps))
    return lax.ppermute(value, axis, [(source, source + steps) for source in range(initial, last)])


def row_norm(values, gain_row):
    return (
        values * lax.rsqrt(jnp.mean(values * values, axis=-1, keepdims=True) + epsilon) * gain_row
    )


def attend(q_lat, cache_rows, new_rows, length, score_scale):
    piece_list = q_lat.shape[0]
    context = cache_rows.shape[0]
    key_rows = jnp.concatenate([cache_rows, new_rows], axis=0)
    scores = (
        jnp.einsum("thl,kl->thk", q_lat, key_rows, preferred_element_type=jnp.float32) * score_scale
    )
    position = lax.broadcasted_iota(jnp.int32, (piece_list, context + piece_list), 1)
    query_pos = lax.broadcasted_iota(jnp.int32, (piece_list, context + piece_list), 0)
    visible = jnp.where(position < context, position < length, position - context <= query_pos)
    scores = jnp.where(visible[:, None, :], scores, -jnp.inf)
    row_max = jnp.max(scores, axis=-1, keepdims=True)
    expd = jnp.where(visible[:, None, :], jnp.exp(scores - row_max), 0.0)
    attention = (expd / jnp.sum(expd, axis=-1, keepdims=True)).astype(jnp.bfloat16)
    return jnp.einsum(
        "thk,kl->thl", attention, key_rows, preferred_element_type=jnp.float32
    ).astype(jnp.bfloat16)


def shards(
    opening_residual,
    incoming_residual,
    stored_summaries,
    stored_counts,
    picked_specialists,
    chooser_mixing_share,
    mixing_scale_factor,
    asking_projection,
    summary_lookup_factor,
    summary_content_factor,
    merging_projection,
    compress_projection,
    summary_scale_factor,
    specialist_scale_factor,
    specialist_switch_factor,
    specialist_widen_factor,
    specialist_contract_factor,
):
    segment_ordinal = lax.axis_index("section")
    section_count = lax.axis_size("section")
    sources = lax.axis_size("expert")
    tick_count = stored_summaries.shape[0]
    piece_list = opening_residual.shape[1]
    inner_feature_midcount = opening_residual.shape[2]
    full_width = mixing_scale_factor.shape[1]
    local_heads = summary_lookup_factor.shape[1]
    head_size = summary_lookup_factor.shape[2]
    top_count = picked_specialists.shape[3]
    expert_local = specialist_switch_factor.shape[1]
    score_scale = head_size ** (-0.5)
    expert_ids = lax.broadcasted_iota(jnp.int32, (1, 1, 1, expert_local * sources), 3)
    shares_dense = jnp.sum(
        jnp.where(
            picked_specialists[:, 0][..., None] == expert_ids,
            chooser_mixing_share[:, 0][..., None],
            0.0,
        ),
        axis=2,
    )
    shares_all = lax.all_gather(
        jnp.swapaxes(shares_dense, 1, 2), "expert", axis=1, tiled=False
    )
    mine = lax.dynamic_slice_in_dim(
        shares_all, lax.axis_index("expert") * expert_local, expert_local, axis=2
    )
    chosen = mine > 0.0
    earlier_or_same = (
        lax.broadcasted_iota(jnp.int32, (piece_list, piece_list), 0)
        <= lax.broadcasted_iota(jnp.int32, (piece_list, piece_list), 1)
    ).astype(jnp.bfloat16)
    rank = jnp.einsum(
        "tjer,rq->tjeq",
        chosen.astype(jnp.bfloat16),
        earlier_or_same,
        preferred_element_type=jnp.float32,
    ).astype(jnp.int32)
    slots = lax.broadcasted_iota(jnp.int32, (1, 1, 1, CAP, 1), 3) + 1
    at_slot = (rank[..., None, :] == slots) & chosen[..., None, :]
    placed = at_slot.astype(jnp.bfloat16)
    slot_share = jnp.sum(jnp.where(at_slot, mine[..., None, :], 0.0), axis=-1)
    outputs = []
    present_carry = opening_residual[0]
    section_out = present_carry
    for step_index in range(tick_count):
        if step_index > 0:
            handed = shifted(section_out, "section", 1)
            present_carry = jnp.where(
                segment_ordinal == 0, incoming_residual[step_index - 1], handed
            )
        micro_index = step_index - segment_ordinal + section_count - 1
        length = lax.dynamic_index_in_dim(stored_counts[:, 0], micro_index, 0, keepdims=False)
        full_rows = lax.all_gather(present_carry, "tensor", axis=1, tiled=True)
        normed = row_norm(full_rows.astype(jnp.float32), mixing_scale_factor[0]).astype(
            jnp.bfloat16
        )
        queries = jnp.dot(normed, asking_projection[0], preferred_element_type=jnp.float32).astype(
            jnp.bfloat16
        )
        queries = queries.reshape(piece_list, local_heads, head_size)
        q_lat = jnp.einsum(
            "thd,hdl->thl", queries, summary_lookup_factor[0], preferred_element_type=jnp.float32
        ).astype(jnp.bfloat16)
        latent_part = jnp.dot(normed, compress_projection[0], preferred_element_type=jnp.float32)
        latent_raw = lax.all_gather(
            latent_part.astype(jnp.bfloat16), "tensor", axis=1, tiled=True
        ).astype(latent_part.dtype)
        new_latent = row_norm(latent_raw, summary_scale_factor[0]).astype(jnp.bfloat16)
        o_lat = attend(q_lat, stored_summaries[step_index, 0, 0], new_latent, length, score_scale)
        heads_out = jnp.einsum(
            "thl,hld->thd", o_lat, summary_content_factor[0], preferred_element_type=jnp.float32
        ).astype(jnp.bfloat16)
        heads_out = heads_out.reshape(piece_list, local_heads * head_size)
        head_terms = jnp.dot(heads_out, merging_projection[0], preferred_element_type=jnp.float32)
        residual = present_carry.astype(jnp.float32) + lax.psum_scatter(
            head_terms.astype(jnp.bfloat16), "tensor", scatter_dimension=1, tiled=True
        ).astype(jnp.float32)
        squares = lax.psum(jnp.sum(residual * residual, axis=1), "tensor")
        moe_input = (
            residual
            * lax.rsqrt(squares / full_width + epsilon)[:, None]
            * specialist_scale_factor[0]
        ).astype(jnp.bfloat16)
        whole_rows = lax.all_gather(moe_input, "tensor", axis=1, tiled=True)
        place = placed[step_index]
        share = slot_share[step_index]
        all_rows = spread(whole_rows)
        hidden_list = []
        for e in range(expert_local):
            rows_in = jnp.einsum(
                "jsr,jrd->jsd", place[:, e], all_rows, preferred_element_type=jnp.float32
            ).astype(jnp.bfloat16)
            rows_in = rows_in.reshape(sources * CAP, full_width)
            gate_values = jnp.dot(
                rows_in, specialist_switch_factor[0, e], preferred_element_type=jnp.float32
            )
            up_values = jnp.dot(
                rows_in, specialist_widen_factor[0, e], preferred_element_type=jnp.float32
            )
            hidden_list.append(
                (jax.nn.silu(gate_values) * up_values * share[:, e].reshape(-1, 1)).astype(
                    jnp.bfloat16
                )
            )
        chunk = full_width // RETURN_CHUNKS
        routed_list = []
        for c in range(RETURN_CHUNKS):
            total = None
            for e in range(expert_local):
                down = jnp.dot(
                    hidden_list[e],
                    specialist_contract_factor[0, e][:, c * chunk : (c + 1) * chunk],
                    preferred_element_type=jnp.float32,
                ).astype(jnp.bfloat16)
                term = jnp.einsum(
                    "jsr,jsd->jrd",
                    place[:, e],
                    down.reshape(sources, CAP, chunk),
                    preferred_element_type=jnp.float32,
                )
                total = term if total is None else total + term
            routed_list.append(gather_sum(total.astype(jnp.bfloat16)))
        routed = jnp.concatenate(routed_list, axis=1)
        routed = lax.psum_scatter(routed, "tensor", scatter_dimension=1, tiled=True).astype(
            jnp.float32
        )
        section_out = (residual + routed).astype(jnp.bfloat16)
        outputs.append(section_out)
    return jnp.stack(outputs)[:, None]


def solution(mesh):
    in_specs = (
        P("section", ("groups", "expert"), "tensor"),
        P(None, ("groups", "expert"), "tensor"),
        P(None, "section", ("groups", "expert"), None, None),
        P(None, ("groups", "expert")),
        P(None, "section", ("groups", "expert"), None),
        P(None, "section", ("groups", "expert"), None),
        P("section", None),
        P("section", None, "tensor"),
        P("section", "tensor", None, None),
        P("section", "tensor", None, None),
        P("section", "tensor", None),
        P("section", None, "tensor"),
        P("section", None),
        P("section", "tensor"),
        P("section", "expert", None, "tensor"),
        P("section", "expert", None, "tensor"),
        P("section", "expert", "tensor", None),
    )
    out_specs = P(None, "section", ("groups", "expert"), "tensor")
    return jax.shard_map(shards, mesh=mesh, in_specs=in_specs, out_specs=out_specs, check_vma=False)
```

```python
import jax
import jax.numpy as jnp
from jax import lax
from jax.experimental import pallas as pl
from jax.experimental.pallas import tpu as pltpu
from jax.sharding import PartitionSpec as P

CAP = 64
RETURN_CHUNKS = 2


epsilon = 1e-06


MESH = pl.DeviceIdType.MESH
PIECES = 2


def place_on_line():
    count = lax.axis_size("expert")
    pair = 2 if count % 2 == 0 else 1
    mine = lax.axis_index("expert")
    return count // pair, pair, mine, mine // pair, lax.rem(mine, pair)


def greet(chips, pair, mine, spot, side):
    barrier = pltpu.get_barrier_semaphore()

    def hello(other):
        pl.semaphore_signal(barrier, inc=1, device_id={"expert": other}, device_id_type=MESH)

    @pl.when(spot > 0)
    def _():
        hello(mine - pair)

    @pl.when(spot < chips - 1)
    def _():
        hello(mine + pair)

    if pair == 2:
        hello(mine + 1 - 2 * side)
    inner = (spot > 0) & (spot < chips - 1)

    @pl.when(inner)
    def _():
        pl.semaphore_wait(barrier, pair + 1)

    @pl.when(jnp.logical_not(inner))
    def _():
        pl.semaphore_wait(barrier, pair)


def remote(src, dst, send, recv, other):
    return pltpu.make_async_remote_copy(
        src_ref=src,
        dst_ref=dst,
        send_sem=send,
        recv_sem=recv,
        device_id={"expert": other},
        device_id_type=MESH,
    )


def spread_kernel(
    own_ref, small_ref, all_ref, small_all_ref, own_sem, line_send, line_recv, side_send, side_recv
):
    chips, pair, mine, spot, side = place_on_line()
    step = own_ref.shape[0] // PIECES
    sibling = mine + 1 - 2 * side

    def rows(block, core, piece):
        if piece == PIECES:
            return small_all_ref.at[block, core]
        return all_ref.at[block, core, pl.ds(piece * step, step)]

    def origin(block, piece):
        if block is not None:
            return rows(block, side, piece)
        return small_ref if piece == PIECES else own_ref.at[pl.ds(piece * step, step)]

    def line_copy(block, piece, way):
        source = origin(block, piece)
        where = spot if block is None else block
        direction = 0 if way > 0 else 1
        return remote(
            source,
            rows(where, side, piece),
            line_send.at[direction, where, piece],
            line_recv.at[where, piece],
            mine + way * pair,
        )

    def side_copy(block, piece):
        source = origin(block, piece)
        where = spot if block is None else block
        return remote(
            source,
            rows(where, side, piece),
            side_send.at[where, piece],
            side_recv.at[where, piece],
            sibling,
        )

    def onward(block, piece, way, act):
        @pl.when((spot < chips - 1) if way > 0 else (spot > 0))
        def _():
            act(line_copy(block, piece, way))

    greet(chips, pair, mine, spot, side)
    for piece in range(PIECES + 1):
        for way in (1, -1):
            onward(None, piece, way, lambda copy: copy.start())
    for piece in range(PIECES + 1):
        if pair == 2:
            side_copy(None, piece).start()
    keep = pltpu.make_async_copy(own_ref, all_ref.at[spot, side], own_sem.at[0])
    keep.start()
    keep_small = pltpu.make_async_copy(small_ref, small_all_ref.at[spot, side], own_sem.at[1])
    keep_small.start()
    for far in range(1, chips):
        for piece in range(PIECES + 1):
            for way in (1, -1):
                block = spot - way * far

                @pl.when((block >= 0) if way > 0 else (block < chips))
                def _():
                    line_copy(block, piece, way).wait_recv()
                    onward(block, piece, way, lambda copy: copy.start())
                    if pair == 2:
                        side_copy(block, piece).start()

    keep.wait()
    keep_small.wait()
    for piece in range(PIECES + 1):
        for way in (1, -1):
            onward(None, piece, way, lambda copy: copy.wait_send())
        if pair == 2:
            side_copy(None, piece).wait()
    for far in range(1, chips):
        for piece in range(PIECES + 1):
            for way in (1, -1):
                block = spot - way * far

                @pl.when((block >= 0) if way > 0 else (block < chips))
                def _():
                    onward(block, piece, way, lambda copy: copy.wait_send())
                    if pair == 2:
                        side_copy(block, piece).wait()


def spread(own, small):
    count = lax.axis_size("expert")
    pair = 2 if count % 2 == 0 else 1
    chips = count // pair
    result, small_result = pl.pallas_call(
        spread_kernel,
        out_shape=[
            jax.ShapeDtypeStruct((chips, pair) + own.shape, own.dtype),
            jax.ShapeDtypeStruct((chips, pair) + small.shape, small.dtype),
        ],
        in_specs=[pl.BlockSpec(memory_space=pltpu.VMEM)] * 2,
        out_specs=[pl.BlockSpec(memory_space=pltpu.VMEM)] * 2,
        scratch_shapes=[
            pltpu.SemaphoreType.DMA((2,)),
            pltpu.SemaphoreType.DMA((2, chips, PIECES + 1)),
            pltpu.SemaphoreType.DMA((chips, PIECES + 1)),
            pltpu.SemaphoreType.DMA((chips, PIECES + 1)),
            pltpu.SemaphoreType.DMA((chips, PIECES + 1)),
        ],
        compiler_params=pltpu.CompilerParams(collective_id=0, has_side_effects=True),
    )(own, small)
    return result.reshape((count,) + own.shape), small_result.reshape((count,) + small.shape)


def gather_sum_kernel(*refs):
    part_refs, refs = refs[:RETURN_CHUNKS], refs[RETURN_CHUNKS:]
    sum_ref, side_in, total, line_in, side_send, side_recv, line_send, line_recv = refs
    chips, pair, mine, spot, side = place_on_line()
    chunk = part_refs[0].shape[3]
    sibling = mine + 1 - 2 * side

    def side_copy(block, piece):
        return remote(
            part_refs[piece].at[block, 1 - side],
            side_in.at[block, piece],
            side_send.at[block, piece],
            side_recv.at[block, piece],
            sibling,
        )

    def line_copy(block, piece, way):
        direction = 0 if way > 0 else 1
        return remote(
            total.at[block, piece],
            line_in.at[direction, block, piece],
            line_send.at[block, piece],
            line_recv.at[direction, block, piece],
            mine + way * pair,
        )

    def wide(value):
        return value.astype(jnp.float32)

    def chip_sum(block, piece):
        value = wide(part_refs[piece][block, side])
        if pair == 2:
            side_copy(block, piece).wait_recv()
            value = value + wide(side_in[block, piece])
        return value

    greet(chips, pair, mine, spot, side)
    if pair == 2:
        for far in range(chips - 1, -1, -1):
            for piece in range(RETURN_CHUNKS):
                for way in (1, -1) if far else (1,):
                    block = spot + way * far

                    @pl.when((block >= 0) & (block < chips))
                    def _():
                        side_copy(block, piece).start()

    for far in range(chips - 1, 0, -1):
        for piece in range(RETURN_CHUNKS):
            for way in (1, -1):
                block = spot + way * far

                @pl.when((block >= 0) & (block < chips))
                def _():
                    value = chip_sum(block, piece)
                    total[block, piece] = value.astype(total.dtype)
                    if far < chips - 1:

                        @pl.when((spot > 0) if way > 0 else (spot < chips - 1))
                        def _():
                            direction = 0 if way > 0 else 1
                            line_copy(block, piece, way).wait_recv()
                            total[block, piece] = (
                                wide(total[block, piece])
                                + wide(line_in[direction, block, piece])
                            ).astype(total.dtype)

                    line_copy(block, piece, way).start()

    for piece in range(RETURN_CHUNKS):
        total[spot, piece] = chip_sum(spot, piece).astype(total.dtype)
        for way in (1, -1):

            @pl.when((spot > 0) if way > 0 else (spot < chips - 1))
            def _():
                direction = 0 if way > 0 else 1
                line_copy(spot, piece, way).wait_recv()
                total[spot, piece] = (
                    wide(total[spot, piece]) + wide(line_in[direction, spot, piece])
                ).astype(total.dtype)

        sum_ref[:, pl.ds(piece * chunk, chunk)] = total[spot, piece]
    for far in range(chips - 1, -1, -1):
        for piece in range(RETURN_CHUNKS):
            for way in (1, -1) if far else (1,):
                block = spot + way * far

                @pl.when((block >= 0) & (block < chips))
                def _():
                    if far:
                        line_copy(block, piece, way).wait_send()
                    if pair == 2:
                        side_copy(block, piece).wait_send()


def gather_sum(parts):
    count, height, chunk = parts[0].shape
    pieces = len(parts)
    kind = parts[0].dtype
    pair = 2 if count % 2 == 0 else 1
    chips = count // pair
    return pl.pallas_call(
        gather_sum_kernel,
        out_shape=jax.ShapeDtypeStruct((height, pieces * chunk), kind),
        in_specs=[pl.BlockSpec(memory_space=pltpu.VMEM)] * pieces,
        out_specs=pl.BlockSpec(memory_space=pltpu.VMEM),
        scratch_shapes=[
            pltpu.VMEM((chips, pieces, height, chunk), kind),
            pltpu.VMEM((chips, pieces, height, chunk), kind),
            pltpu.VMEM((2, chips, pieces, height, chunk), kind),
            pltpu.SemaphoreType.DMA((chips, pieces)),
            pltpu.SemaphoreType.DMA((chips, pieces)),
            pltpu.SemaphoreType.DMA((chips, pieces)),
            pltpu.SemaphoreType.DMA((2, chips, pieces)),
        ],
        compiler_params=pltpu.CompilerParams(collective_id=1, has_side_effects=True),
    )(*[part.reshape(chips, pair, height, chunk) for part in parts])


def shifted(value, axis, steps):
    count = lax.axis_size(axis)
    initial, last = (max(0, -steps), min(count, count - steps))
    return lax.ppermute(value, axis, [(source, source + steps) for source in range(initial, last)])


def row_norm(values, gain_row):
    return (
        values * lax.rsqrt(jnp.mean(values * values, axis=-1, keepdims=True) + epsilon) * gain_row
    )


def attend(q_lat, cache_rows, new_rows, length, score_scale):
    piece_list = q_lat.shape[0]
    context = cache_rows.shape[0]
    key_rows = jnp.concatenate([cache_rows, new_rows], axis=0)
    scores = (
        jnp.einsum("thl,kl->thk", q_lat, key_rows, preferred_element_type=jnp.float32) * score_scale
    )
    position = lax.broadcasted_iota(jnp.int32, (piece_list, context + piece_list), 1)
    query_pos = lax.broadcasted_iota(jnp.int32, (piece_list, context + piece_list), 0)
    visible = jnp.where(position < context, position < length, position - context <= query_pos)
    scores = jnp.where(visible[:, None, :], scores, -jnp.inf)
    row_max = jnp.max(scores, axis=-1, keepdims=True)
    expd = jnp.where(visible[:, None, :], jnp.exp(scores - row_max), 0.0)
    attention = (expd / jnp.sum(expd, axis=-1, keepdims=True)).astype(jnp.bfloat16)
    return jnp.einsum(
        "thk,kl->thl", attention, key_rows, preferred_element_type=jnp.float32
    ).astype(jnp.bfloat16)


def shards(
    opening_residual,
    incoming_residual,
    stored_summaries,
    stored_counts,
    picked_specialists,
    chooser_mixing_share,
    mixing_scale_factor,
    asking_projection,
    summary_lookup_factor,
    summary_content_factor,
    merging_projection,
    compress_projection,
    summary_scale_factor,
    specialist_scale_factor,
    specialist_switch_factor,
    specialist_widen_factor,
    specialist_contract_factor,
):
    segment_ordinal = lax.axis_index("section")
    section_count = lax.axis_size("section")
    sources = lax.axis_size("expert")
    tick_count = stored_summaries.shape[0]
    piece_list = opening_residual.shape[1]
    inner_feature_midcount = opening_residual.shape[2]
    full_width = mixing_scale_factor.shape[1]
    local_heads = summary_lookup_factor.shape[1]
    head_size = summary_lookup_factor.shape[2]
    top_count = picked_specialists.shape[3]
    expert_local = specialist_switch_factor.shape[1]
    score_scale = head_size ** (-0.5)
    expert_ids = lax.broadcasted_iota(jnp.int32, (1, 1, 1, expert_local * sources), 3)
    shares_dense = jnp.sum(
        jnp.where(
            picked_specialists[:, 0][..., None] == expert_ids,
            chooser_mixing_share[:, 0][..., None],
            0.0,
        ),
        axis=2,
    )
    shares_dense = jnp.swapaxes(shares_dense, 1, 2)
    earlier_or_same = (
        lax.broadcasted_iota(jnp.int32, (piece_list, piece_list), 0)
        <= lax.broadcasted_iota(jnp.int32, (piece_list, piece_list), 1)
    ).astype(jnp.bfloat16)
    slots = lax.broadcasted_iota(jnp.int32, (1, 1, CAP, 1), 2) + 1
    outputs = []
    present_carry = opening_residual[0]
    section_out = present_carry
    for step_index in range(tick_count):
        if step_index > 0:
            handed = shifted(section_out, "section", 1)
            present_carry = jnp.where(
                segment_ordinal == 0, incoming_residual[step_index - 1], handed
            )
        micro_index = step_index - segment_ordinal + section_count - 1
        length = lax.dynamic_index_in_dim(stored_counts[:, 0], micro_index, 0, keepdims=False)
        full_rows = lax.all_gather(present_carry, "tensor", axis=1, tiled=True)
        normed = row_norm(full_rows.astype(jnp.float32), mixing_scale_factor[0]).astype(
            jnp.bfloat16
        )
        queries = jnp.dot(normed, asking_projection[0], preferred_element_type=jnp.float32).astype(
            jnp.bfloat16
        )
        queries = queries.reshape(piece_list, local_heads, head_size)
        q_lat = jnp.einsum(
            "thd,hdl->thl", queries, summary_lookup_factor[0], preferred_element_type=jnp.float32
        ).astype(jnp.bfloat16)
        latent_part = jnp.dot(normed, compress_projection[0], preferred_element_type=jnp.float32)
        latent_raw = lax.all_gather(
            latent_part.astype(jnp.bfloat16), "tensor", axis=1, tiled=True
        ).astype(latent_part.dtype)
        new_latent = row_norm(latent_raw, summary_scale_factor[0]).astype(jnp.bfloat16)
        o_lat = attend(q_lat, stored_summaries[step_index, 0, 0], new_latent, length, score_scale)
        heads_out = jnp.einsum(
            "thl,hld->thd", o_lat, summary_content_factor[0], preferred_element_type=jnp.float32
        ).astype(jnp.bfloat16)
        heads_out = heads_out.reshape(piece_list, local_heads * head_size)
        head_terms = jnp.dot(heads_out, merging_projection[0], preferred_element_type=jnp.float32)
        residual = present_carry.astype(jnp.float32) + lax.psum_scatter(
            head_terms.astype(jnp.bfloat16), "tensor", scatter_dimension=1, tiled=True
        ).astype(jnp.float32)
        squares = lax.psum(jnp.sum(residual * residual, axis=1), "tensor")
        moe_input = (
            residual
            * lax.rsqrt(squares / full_width + epsilon)[:, None]
            * specialist_scale_factor[0]
        ).astype(jnp.bfloat16)
        whole_rows = lax.all_gather(moe_input, "tensor", axis=1, tiled=True)
        all_rows, all_shares = spread(whole_rows, shares_dense[step_index])
        mine = lax.dynamic_slice_in_dim(
            all_shares, lax.axis_index("expert") * expert_local, expert_local, axis=1
        )
        chosen = mine > 0.0
        rank = jnp.einsum(
            "jer,rq->jeq",
            chosen.astype(jnp.bfloat16),
            earlier_or_same,
            preferred_element_type=jnp.float32,
        ).astype(jnp.int32)
        at_slot = (rank[..., None, :] == slots) & chosen[..., None, :]
        place = at_slot.astype(jnp.bfloat16)
        share = jnp.sum(jnp.where(at_slot, mine[..., None, :], 0.0), axis=-1)
        hidden_list = []
        for e in range(expert_local):
            rows_in = jnp.einsum(
                "jsr,jrd->jsd", place[:, e], all_rows, preferred_element_type=jnp.float32
            ).astype(jnp.bfloat16)
            rows_in = rows_in.reshape(sources * CAP, full_width)
            gate_values = jnp.dot(
                rows_in, specialist_switch_factor[0, e], preferred_element_type=jnp.float32
            )
            up_values = jnp.dot(
                rows_in, specialist_widen_factor[0, e], preferred_element_type=jnp.float32
            )
            hidden_list.append(
                (jax.nn.silu(gate_values) * up_values * share[:, e].reshape(-1, 1)).astype(
                    jnp.bfloat16
                )
            )
        chunk = full_width // RETURN_CHUNKS
        routed_list = []
        for c in range(RETURN_CHUNKS):
            total = None
            for e in range(expert_local):
                down = jnp.dot(
                    hidden_list[e],
                    specialist_contract_factor[0, e][:, c * chunk : (c + 1) * chunk],
                    preferred_element_type=jnp.float32,
                ).astype(jnp.bfloat16)
                term = jnp.einsum(
                    "jsr,jsd->jrd",
                    place[:, e],
                    down.reshape(sources, CAP, chunk),
                    preferred_element_type=jnp.float32,
                )
                total = term if total is None else total + term
            routed_list.append(total.astype(jnp.bfloat16))
        routed = gather_sum(routed_list)
        routed = lax.psum_scatter(routed, "tensor", scatter_dimension=1, tiled=True).astype(
            jnp.float32
        )
        section_out = (residual + routed).astype(jnp.bfloat16)
        outputs.append(section_out)
    return jnp.stack(outputs)[:, None]


def solution(mesh):
    in_specs = (
        P("section", ("groups", "expert"), "tensor"),
        P(None, ("groups", "expert"), "tensor"),
        P(None, "section", ("groups", "expert"), None, None),
        P(None, ("groups", "expert")),
        P(None, "section", ("groups", "expert"), None),
        P(None, "section", ("groups", "expert"), None),
        P("section", None),
        P("section", None, "tensor"),
        P("section", "tensor", None, None),
        P("section", "tensor", None, None),
        P("section", "tensor", None),
        P("section", None, "tensor"),
        P("section", None),
        P("section", "tensor"),
        P("section", "expert", None, "tensor"),
        P("section", "expert", None, "tensor"),
        P("section", "expert", "tensor", None),
    )
    out_specs = P(None, "section", ("groups", "expert"), "tensor")
    return jax.shard_map(shards, mesh=mesh, in_specs=in_specs, out_specs=out_specs, check_vma=False)
```

```python
import jax
import jax.numpy as jnp
from jax import lax
from jax.experimental import pallas as pl
from jax.experimental.pallas import tpu as pltpu
from jax.sharding import PartitionSpec as P

CAP = 64
RETURN_CHUNKS = 2


epsilon = 1e-06


MESH = pl.DeviceIdType.MESH
PIECES = 2


def place_on_line():
    count = lax.axis_size("expert")
    pair = 2 if count % 2 == 0 else 1
    mine = lax.axis_index("expert")
    return count // pair, pair, mine, mine // pair, lax.rem(mine, pair)


def greet(chips, pair, mine, spot, side):
    barrier = pltpu.get_barrier_semaphore()

    def hello(other):
        pl.semaphore_signal(barrier, inc=1, device_id={"expert": other}, device_id_type=MESH)

    @pl.when(spot > 0)
    def _():
        hello(mine - pair)

    @pl.when(spot < chips - 1)
    def _():
        hello(mine + pair)

    if pair == 2:
        hello(mine + 1 - 2 * side)
    inner = (spot > 0) & (spot < chips - 1)

    @pl.when(inner)
    def _():
        pl.semaphore_wait(barrier, pair + 1)

    @pl.when(jnp.logical_not(inner))
    def _():
        pl.semaphore_wait(barrier, pair)


def remote(src, dst, send, recv, other):
    return pltpu.make_async_remote_copy(
        src_ref=src,
        dst_ref=dst,
        send_sem=send,
        recv_sem=recv,
        device_id={"expert": other},
        device_id_type=MESH,
    )


def spread_kernel(
    own_ref, small_ref, all_ref, small_all_ref, own_sem, line_send, line_recv, side_send, side_recv
):
    chips, pair, mine, spot, side = place_on_line()
    step = own_ref.shape[0] // PIECES
    sibling = mine + 1 - 2 * side

    def rows(block, core, piece):
        if piece == PIECES:
            return small_all_ref.at[block, core]
        return all_ref.at[block, core, pl.ds(piece * step, step)]

    def origin(block, piece):
        if block is not None:
            return rows(block, side, piece)
        return small_ref if piece == PIECES else own_ref.at[pl.ds(piece * step, step)]

    def line_copy(block, piece, way):
        source = origin(block, piece)
        where = spot if block is None else block
        direction = 0 if way > 0 else 1
        return remote(
            source,
            rows(where, side, piece),
            line_send.at[direction, where, piece],
            line_recv.at[where, piece],
            mine + way * pair,
        )

    def side_copy(block, piece):
        source = origin(block, piece)
        where = spot if block is None else block
        return remote(
            source,
            rows(where, side, piece),
            side_send.at[where, piece],
            side_recv.at[where, piece],
            sibling,
        )

    def onward(block, piece, way, act):
        @pl.when((spot < chips - 1) if way > 0 else (spot > 0))
        def _():
            act(line_copy(block, piece, way))

    greet(chips, pair, mine, spot, side)
    for piece in range(PIECES + 1):
        for way in (1, -1):
            onward(None, piece, way, lambda copy: copy.start())
    for piece in range(PIECES + 1):
        if pair == 2:
            side_copy(None, piece).start()
    keep = pltpu.make_async_copy(own_ref, all_ref.at[spot, side], own_sem.at[0])
    keep.start()
    keep_small = pltpu.make_async_copy(small_ref, small_all_ref.at[spot, side], own_sem.at[1])
    keep_small.start()
    for far in range(1, chips):
        for piece in range(PIECES + 1):
            for way in (1, -1):
                block = spot - way * far

                @pl.when((block >= 0) if way > 0 else (block < chips))
                def _():
                    line_copy(block, piece, way).wait_recv()
                    onward(block, piece, way, lambda copy: copy.start())
                    if pair == 2:
                        side_copy(block, piece).start()

    keep.wait()
    keep_small.wait()
    for piece in range(PIECES + 1):
        for way in (1, -1):
            onward(None, piece, way, lambda copy: copy.wait_send())
        if pair == 2:
            side_copy(None, piece).wait()
    for far in range(1, chips):
        for piece in range(PIECES + 1):
            for way in (1, -1):
                block = spot - way * far

                @pl.when((block >= 0) if way > 0 else (block < chips))
                def _():
                    onward(block, piece, way, lambda copy: copy.wait_send())
                    if pair == 2:
                        side_copy(block, piece).wait()


def spread(own, small):
    count = lax.axis_size("expert")
    pair = 2 if count % 2 == 0 else 1
    chips = count // pair
    held = count * own.size * own.dtype.itemsize
    result, small_result = pl.pallas_call(
        spread_kernel,
        out_shape=[
            jax.ShapeDtypeStruct((chips, pair) + own.shape, own.dtype),
            jax.ShapeDtypeStruct((chips, pair) + small.shape, small.dtype),
        ],
        in_specs=[pl.BlockSpec(memory_space=pltpu.VMEM)] * 2,
        out_specs=[pl.BlockSpec(memory_space=pltpu.VMEM)] * 2,
        scratch_shapes=[
            pltpu.SemaphoreType.DMA((2,)),
            pltpu.SemaphoreType.DMA((2, chips, PIECES + 1)),
            pltpu.SemaphoreType.DMA((chips, PIECES + 1)),
            pltpu.SemaphoreType.DMA((chips, PIECES + 1)),
            pltpu.SemaphoreType.DMA((chips, PIECES + 1)),
        ],
        compiler_params=pltpu.CompilerParams(
            collective_id=0, has_side_effects=True, vmem_limit_bytes=2 * held
        ),
        cost_estimate=pl.CostEstimate(flops=0, bytes_accessed=32 * held, transcendentals=0),
    )(own, small)
    return result.reshape((count,) + own.shape), small_result.reshape((count,) + small.shape)


def gather_sum_kernel(*refs):
    part_refs, refs = refs[:RETURN_CHUNKS], refs[RETURN_CHUNKS:]
    sum_ref, side_in, total, line_in, side_send, side_recv, line_send, line_recv = refs
    chips, pair, mine, spot, side = place_on_line()
    chunk = part_refs[0].shape[3]
    sibling = mine + 1 - 2 * side

    def side_copy(block, piece):
        return remote(
            part_refs[piece].at[block, 1 - side],
            side_in.at[block, piece],
            side_send.at[block, piece],
            side_recv.at[block, piece],
            sibling,
        )

    def line_copy(block, piece, way):
        direction = 0 if way > 0 else 1
        return remote(
            total.at[block, piece],
            line_in.at[direction, block, piece],
            line_send.at[block, piece],
            line_recv.at[direction, block, piece],
            mine + way * pair,
        )

    def wide(value):
        return value.astype(jnp.float32)

    def chip_sum(block, piece):
        value = wide(part_refs[piece][block, side])
        if pair == 2:
            side_copy(block, piece).wait_recv()
            value = value + wide(side_in[block, piece])
        return value

    greet(chips, pair, mine, spot, side)
    if pair == 2:
        for far in range(chips - 1, -1, -1):
            for piece in range(RETURN_CHUNKS):
                for way in (1, -1) if far else (1,):
                    block = spot + way * far

                    @pl.when((block >= 0) & (block < chips))
                    def _():
                        side_copy(block, piece).start()

    for far in range(chips - 1, 0, -1):
        for piece in range(RETURN_CHUNKS):
            for way in (1, -1):
                block = spot + way * far

                @pl.when((block >= 0) & (block < chips))
                def _():
                    value = chip_sum(block, piece)
                    total[block, piece] = value.astype(total.dtype)
                    if far < chips - 1:

                        @pl.when((spot > 0) if way > 0 else (spot < chips - 1))
                        def _():
                            direction = 0 if way > 0 else 1
                            line_copy(block, piece, way).wait_recv()
                            total[block, piece] = (
                                wide(total[block, piece])
                                + wide(line_in[direction, block, piece])
                            ).astype(total.dtype)

                    line_copy(block, piece, way).start()

    for piece in range(RETURN_CHUNKS):
        total[spot, piece] = chip_sum(spot, piece).astype(total.dtype)
        for way in (1, -1):

            @pl.when((spot > 0) if way > 0 else (spot < chips - 1))
            def _():
                direction = 0 if way > 0 else 1
                line_copy(spot, piece, way).wait_recv()
                total[spot, piece] = (
                    wide(total[spot, piece]) + wide(line_in[direction, spot, piece])
                ).astype(total.dtype)

        sum_ref[:, pl.ds(piece * chunk, chunk)] = total[spot, piece]
    for far in range(chips - 1, -1, -1):
        for piece in range(RETURN_CHUNKS):
            for way in (1, -1) if far else (1,):
                block = spot + way * far

                @pl.when((block >= 0) & (block < chips))
                def _():
                    if far:
                        line_copy(block, piece, way).wait_send()
                    if pair == 2:
                        side_copy(block, piece).wait_send()


def gather_sum(parts):
    count, height, chunk = parts[0].shape
    pieces = len(parts)
    kind = parts[0].dtype
    held = pieces * parts[0].size * kind.itemsize
    pair = 2 if count % 2 == 0 else 1
    chips = count // pair
    return pl.pallas_call(
        gather_sum_kernel,
        out_shape=jax.ShapeDtypeStruct((height, pieces * chunk), kind),
        in_specs=[pl.BlockSpec(memory_space=pltpu.VMEM)] * pieces,
        out_specs=pl.BlockSpec(memory_space=pltpu.VMEM),
        scratch_shapes=[
            pltpu.VMEM((chips, pieces, height, chunk), kind),
            pltpu.VMEM((chips, pieces, height, chunk), kind),
            pltpu.VMEM((2, chips, pieces, height, chunk), kind),
            pltpu.SemaphoreType.DMA((chips, pieces)),
            pltpu.SemaphoreType.DMA((chips, pieces)),
            pltpu.SemaphoreType.DMA((chips, pieces)),
            pltpu.SemaphoreType.DMA((2, chips, pieces)),
        ],
        compiler_params=pltpu.CompilerParams(
            collective_id=1, has_side_effects=True, vmem_limit_bytes=4 * held
        ),
        cost_estimate=pl.CostEstimate(flops=0, bytes_accessed=32 * held, transcendentals=0),
    )(*[part.reshape(chips, pair, height, chunk) for part in parts])


def shifted(value, axis, steps):
    count = lax.axis_size(axis)
    initial, last = (max(0, -steps), min(count, count - steps))
    return lax.ppermute(value, axis, [(source, source + steps) for source in range(initial, last)])


def row_norm(values, gain_row):
    return (
        values * lax.rsqrt(jnp.mean(values * values, axis=-1, keepdims=True) + epsilon) * gain_row
    )


def attend(q_lat, cache_rows, new_rows, length, score_scale):
    piece_list = q_lat.shape[0]
    context = cache_rows.shape[0]
    key_rows = jnp.concatenate([cache_rows, new_rows], axis=0)
    scores = (
        jnp.einsum("thl,kl->thk", q_lat, key_rows, preferred_element_type=jnp.float32) * score_scale
    )
    position = lax.broadcasted_iota(jnp.int32, (piece_list, context + piece_list), 1)
    query_pos = lax.broadcasted_iota(jnp.int32, (piece_list, context + piece_list), 0)
    visible = jnp.where(position < context, position < length, position - context <= query_pos)
    scores = jnp.where(visible[:, None, :], scores, -jnp.inf)
    row_max = jnp.max(scores, axis=-1, keepdims=True)
    expd = jnp.where(visible[:, None, :], jnp.exp(scores - row_max), 0.0)
    attention = (expd / jnp.sum(expd, axis=-1, keepdims=True)).astype(jnp.bfloat16)
    return jnp.einsum(
        "thk,kl->thl", attention, key_rows, preferred_element_type=jnp.float32
    ).astype(jnp.bfloat16)


def shards(
    opening_residual,
    incoming_residual,
    stored_summaries,
    stored_counts,
    picked_specialists,
    chooser_mixing_share,
    mixing_scale_factor,
    asking_projection,
    summary_lookup_factor,
    summary_content_factor,
    merging_projection,
    compress_projection,
    summary_scale_factor,
    specialist_scale_factor,
    specialist_switch_factor,
    specialist_widen_factor,
    specialist_contract_factor,
):
    segment_ordinal = lax.axis_index("section")
    section_count = lax.axis_size("section")
    sources = lax.axis_size("expert")
    tick_count = stored_summaries.shape[0]
    piece_list = opening_residual.shape[1]
    inner_feature_midcount = opening_residual.shape[2]
    full_width = mixing_scale_factor.shape[1]
    local_heads = summary_lookup_factor.shape[1]
    head_size = summary_lookup_factor.shape[2]
    top_count = picked_specialists.shape[3]
    expert_local = specialist_switch_factor.shape[1]
    score_scale = head_size ** (-0.5)
    expert_ids = lax.broadcasted_iota(jnp.int32, (1, 1, 1, expert_local * sources), 3)
    shares_dense = jnp.sum(
        jnp.where(
            picked_specialists[:, 0][..., None] == expert_ids,
            chooser_mixing_share[:, 0][..., None],
            0.0,
        ),
        axis=2,
    )
    shares_dense = jnp.swapaxes(shares_dense, 1, 2)
    earlier_or_same = (
        lax.broadcasted_iota(jnp.int32, (piece_list, piece_list), 0)
        <= lax.broadcasted_iota(jnp.int32, (piece_list, piece_list), 1)
    ).astype(jnp.bfloat16)
    slots = lax.broadcasted_iota(jnp.int32, (1, 1, CAP, 1), 2) + 1
    outputs = []
    present_carry = opening_residual[0]
    section_out = present_carry
    for step_index in range(tick_count):
        if step_index > 0:
            handed = shifted(section_out, "section", 1)
            present_carry = jnp.where(
                segment_ordinal == 0, incoming_residual[step_index - 1], handed
            )
        micro_index = step_index - segment_ordinal + section_count - 1
        length = lax.dynamic_index_in_dim(stored_counts[:, 0], micro_index, 0, keepdims=False)
        full_rows = lax.all_gather(present_carry, "tensor", axis=1, tiled=True)
        normed = row_norm(full_rows.astype(jnp.float32), mixing_scale_factor[0]).astype(
            jnp.bfloat16
        )
        queries = jnp.dot(normed, asking_projection[0], preferred_element_type=jnp.float32).astype(
            jnp.bfloat16
        )
        queries = queries.reshape(piece_list, local_heads, head_size)
        q_lat = jnp.einsum(
            "thd,hdl->thl", queries, summary_lookup_factor[0], preferred_element_type=jnp.float32
        ).astype(jnp.bfloat16)
        latent_part = jnp.dot(normed, compress_projection[0], preferred_element_type=jnp.float32)
        latent_raw = lax.all_gather(
            latent_part.astype(jnp.bfloat16), "tensor", axis=1, tiled=True
        ).astype(latent_part.dtype)
        new_latent = row_norm(latent_raw, summary_scale_factor[0]).astype(jnp.bfloat16)
        o_lat = attend(q_lat, stored_summaries[step_index, 0, 0], new_latent, length, score_scale)
        heads_out = jnp.einsum(
            "thl,hld->thd", o_lat, summary_content_factor[0], preferred_element_type=jnp.float32
        ).astype(jnp.bfloat16)
        heads_out = heads_out.reshape(piece_list, local_heads * head_size)
        head_terms = jnp.dot(heads_out, merging_projection[0], preferred_element_type=jnp.float32)
        residual = present_carry.astype(jnp.float32) + lax.psum_scatter(
            head_terms.astype(jnp.bfloat16), "tensor", scatter_dimension=1, tiled=True
        ).astype(jnp.float32)
        squares = lax.psum(jnp.sum(residual * residual, axis=1), "tensor")
        moe_input = (
            residual
            * lax.rsqrt(squares / full_width + epsilon)[:, None]
            * specialist_scale_factor[0]
        ).astype(jnp.bfloat16)
        whole_rows = lax.all_gather(moe_input, "tensor", axis=1, tiled=True)
        all_rows, all_shares = spread(whole_rows, shares_dense[step_index])
        mine = lax.dynamic_slice_in_dim(
            all_shares, lax.axis_index("expert") * expert_local, expert_local, axis=1
        )
        chosen = mine > 0.0
        rank = jnp.einsum(
            "jer,rq->jeq",
            chosen.astype(jnp.bfloat16),
            earlier_or_same,
            preferred_element_type=jnp.float32,
        ).astype(jnp.int32)
        at_slot = (rank[..., None, :] == slots) & chosen[..., None, :]
        place = at_slot.astype(jnp.bfloat16)
        share = jnp.sum(jnp.where(at_slot, mine[..., None, :], 0.0), axis=-1)
        hidden_list = []
        for e in range(expert_local):
            rows_in = jnp.einsum(
                "jsr,jrd->jsd", place[:, e], all_rows, preferred_element_type=jnp.float32
            ).astype(jnp.bfloat16)
            rows_in = rows_in.reshape(sources * CAP, full_width)
            gate_values = jnp.dot(
                rows_in, specialist_switch_factor[0, e], preferred_element_type=jnp.float32
            )
            up_values = jnp.dot(
                rows_in, specialist_widen_factor[0, e], preferred_element_type=jnp.float32
            )
            hidden_list.append(
                (jax.nn.silu(gate_values) * up_values * share[:, e].reshape(-1, 1)).astype(
                    jnp.bfloat16
                )
            )
        chunk = full_width // RETURN_CHUNKS
        routed_list = []
        for c in range(RETURN_CHUNKS):
            total = None
            for e in range(expert_local):
                down = jnp.dot(
                    hidden_list[e],
                    specialist_contract_factor[0, e][:, c * chunk : (c + 1) * chunk],
                    preferred_element_type=jnp.float32,
                ).astype(jnp.bfloat16)
                term = jnp.einsum(
                    "jsr,jsd->jrd",
                    place[:, e],
                    down.reshape(sources, CAP, chunk),
                    preferred_element_type=jnp.float32,
                )
                total = term if total is None else total + term
            routed_list.append(total.astype(jnp.bfloat16))
        routed = gather_sum(routed_list)
        routed = lax.psum_scatter(routed, "tensor", scatter_dimension=1, tiled=True).astype(
            jnp.float32
        )
        section_out = (residual + routed).astype(jnp.bfloat16)
        outputs.append(section_out)
    return jnp.stack(outputs)[:, None]


def solution(mesh):
    in_specs = (
        P("section", ("groups", "expert"), "tensor"),
        P(None, ("groups", "expert"), "tensor"),
        P(None, "section", ("groups", "expert"), None, None),
        P(None, ("groups", "expert")),
        P(None, "section", ("groups", "expert"), None),
        P(None, "section", ("groups", "expert"), None),
        P("section", None),
        P("section", None, "tensor"),
        P("section", "tensor", None, None),
        P("section", "tensor", None, None),
        P("section", "tensor", None),
        P("section", None, "tensor"),
        P("section", None),
        P("section", "tensor"),
        P("section", "expert", None, "tensor"),
        P("section", "expert", None, "tensor"),
        P("section", "expert", "tensor", None),
    )
    out_specs = P(None, "section", ("groups", "expert"), "tensor")
    return jax.shard_map(shards, mesh=mesh, in_specs=in_specs, out_specs=out_specs, check_vma=False)
```

```python
import jax
import jax.numpy as jnp
from jax import lax
from jax.experimental import pallas as pl
from jax.experimental.pallas import tpu as pltpu
from jax.sharding import PartitionSpec as P

CAP = 64
RETURN_CHUNKS = 2


epsilon = 1e-06


MESH = pl.DeviceIdType.MESH
PIECES = 4


def place_on_line():
    count = lax.axis_size("expert")
    pair = 2 if count % 2 == 0 else 1
    mine = lax.axis_index("expert")
    return count // pair, pair, mine, mine // pair, lax.rem(mine, pair)


def greet(chips, pair, mine, spot, side):
    barrier = pltpu.get_barrier_semaphore()

    def hello(other):
        pl.semaphore_signal(barrier, inc=1, device_id={"expert": other}, device_id_type=MESH)

    @pl.when(spot > 0)
    def _():
        hello(mine - pair)

    @pl.when(spot < chips - 1)
    def _():
        hello(mine + pair)

    if pair == 2:
        hello(mine + 1 - 2 * side)
    inner = (spot > 0) & (spot < chips - 1)

    @pl.when(inner)
    def _():
        pl.semaphore_wait(barrier, pair + 1)

    @pl.when(jnp.logical_not(inner))
    def _():
        pl.semaphore_wait(barrier, pair)


def remote(src, dst, send, recv, other):
    return pltpu.make_async_remote_copy(
        src_ref=src,
        dst_ref=dst,
        send_sem=send,
        recv_sem=recv,
        device_id={"expert": other},
        device_id_type=MESH,
    )


def spread_kernel(
    own_ref, small_ref, all_ref, small_all_ref, own_sem, line_send, line_recv, side_send, side_recv
):
    chips, pair, mine, spot, side = place_on_line()
    step = own_ref.shape[0] // PIECES
    sibling = mine + 1 - 2 * side

    def rows(block, core, piece):
        if piece == PIECES:
            return small_all_ref.at[block, core]
        return all_ref.at[block, core, pl.ds(piece * step, step)]

    def origin(block, piece):
        if block is not None:
            return rows(block, side, piece)
        return small_ref if piece == PIECES else own_ref.at[pl.ds(piece * step, step)]

    def line_copy(block, piece, way):
        source = origin(block, piece)
        where = spot if block is None else block
        direction = 0 if way > 0 else 1
        return remote(
            source,
            rows(where, side, piece),
            line_send.at[direction, where, piece],
            line_recv.at[where, piece],
            mine + way * pair,
        )

    def side_copy(block, piece):
        source = origin(block, piece)
        where = spot if block is None else block
        return remote(
            source,
            rows(where, side, piece),
            side_send.at[where, piece],
            side_recv.at[where, piece],
            sibling,
        )

    def onward(block, piece, way, act):
        @pl.when((spot < chips - 1) if way > 0 else (spot > 0))
        def _():
            act(line_copy(block, piece, way))

    greet(chips, pair, mine, spot, side)
    for piece in range(PIECES + 1):
        for way in (1, -1):
            onward(None, piece, way, lambda copy: copy.start())
    for piece in range(PIECES + 1):
        if pair == 2:
            side_copy(None, piece).start()
    keep = pltpu.make_async_copy(own_ref, all_ref.at[spot, side], own_sem.at[0])
    keep.start()
    keep_small = pltpu.make_async_copy(small_ref, small_all_ref.at[spot, side], own_sem.at[1])
    keep_small.start()
    for far in range(1, chips):
        for piece in range(PIECES + 1):
            for way in (1, -1):
                block = spot - way * far

                @pl.when((block >= 0) if way > 0 else (block < chips))
                def _():
                    line_copy(block, piece, way).wait_recv()
                    onward(block, piece, way, lambda copy: copy.start())
                    if pair == 2:
                        side_copy(block, piece).start()

    keep.wait()
    keep_small.wait()
    for piece in range(PIECES + 1):
        for way in (1, -1):
            onward(None, piece, way, lambda copy: copy.wait_send())
        if pair == 2:
            side_copy(None, piece).wait()
    for far in range(1, chips):
        for piece in range(PIECES + 1):
            for way in (1, -1):
                block = spot - way * far

                @pl.when((block >= 0) if way > 0 else (block < chips))
                def _():
                    onward(block, piece, way, lambda copy: copy.wait_send())
                    if pair == 2:
                        side_copy(block, piece).wait()


def spread(own, small):
    count = lax.axis_size("expert")
    pair = 2 if count % 2 == 0 else 1
    chips = count // pair
    held = count * own.size * own.dtype.itemsize
    result, small_result = pl.pallas_call(
        spread_kernel,
        out_shape=[
            jax.ShapeDtypeStruct((chips, pair) + own.shape, own.dtype),
            jax.ShapeDtypeStruct((chips, pair) + small.shape, small.dtype),
        ],
        in_specs=[pl.BlockSpec(memory_space=pltpu.VMEM)] * 2,
        out_specs=[pl.BlockSpec(memory_space=pltpu.VMEM)] * 2,
        scratch_shapes=[
            pltpu.SemaphoreType.DMA((2,)),
            pltpu.SemaphoreType.DMA((2, chips, PIECES + 1)),
            pltpu.SemaphoreType.DMA((chips, PIECES + 1)),
            pltpu.SemaphoreType.DMA((chips, PIECES + 1)),
            pltpu.SemaphoreType.DMA((chips, PIECES + 1)),
        ],
        compiler_params=pltpu.CompilerParams(
            collective_id=0, has_side_effects=True, vmem_limit_bytes=2 * held
        ),
        cost_estimate=pl.CostEstimate(flops=0, bytes_accessed=32 * held, transcendentals=0),
    )(own, small)
    return result.reshape((count,) + own.shape), small_result.reshape((count,) + small.shape)


def gather_sum_kernel(*refs):
    part_refs, refs = refs[:RETURN_CHUNKS], refs[RETURN_CHUNKS:]
    sum_ref, side_in, total, line_in, side_send, side_recv, line_send, line_recv = refs
    chips, pair, mine, spot, side = place_on_line()
    chunk = part_refs[0].shape[3]
    sibling = mine + 1 - 2 * side

    def side_copy(block, piece):
        return remote(
            part_refs[piece].at[block, 1 - side],
            side_in.at[block, piece],
            side_send.at[block, piece],
            side_recv.at[block, piece],
            sibling,
        )

    def line_copy(block, piece, way):
        direction = 0 if way > 0 else 1
        return remote(
            total.at[block, piece],
            line_in.at[direction, block, piece],
            line_send.at[block, piece],
            line_recv.at[direction, block, piece],
            mine + way * pair,
        )

    def wide(value):
        return value.astype(jnp.float32)

    def chip_sum(block, piece):
        value = wide(part_refs[piece][block, side])
        if pair == 2:
            side_copy(block, piece).wait_recv()
            value = value + wide(side_in[block, piece])
        return value

    greet(chips, pair, mine, spot, side)
    if pair == 2:
        for far in range(chips - 1, -1, -1):
            for piece in range(RETURN_CHUNKS):
                for way in (1, -1) if far else (1,):
                    block = spot + way * far

                    @pl.when((block >= 0) & (block < chips))
                    def _():
                        side_copy(block, piece).start()

    for far in range(chips - 1, 0, -1):
        for piece in range(RETURN_CHUNKS):
            for way in (1, -1):
                block = spot + way * far

                @pl.when((block >= 0) & (block < chips))
                def _():
                    value = chip_sum(block, piece)
                    total[block, piece] = value.astype(total.dtype)
                    if far < chips - 1:

                        @pl.when((spot > 0) if way > 0 else (spot < chips - 1))
                        def _():
                            direction = 0 if way > 0 else 1
                            line_copy(block, piece, way).wait_recv()
                            total[block, piece] = (
                                wide(total[block, piece])
                                + wide(line_in[direction, block, piece])
                            ).astype(total.dtype)

                    line_copy(block, piece, way).start()

    for piece in range(RETURN_CHUNKS):
        total[spot, piece] = chip_sum(spot, piece).astype(total.dtype)
        for way in (1, -1):

            @pl.when((spot > 0) if way > 0 else (spot < chips - 1))
            def _():
                direction = 0 if way > 0 else 1
                line_copy(spot, piece, way).wait_recv()
                total[spot, piece] = (
                    wide(total[spot, piece]) + wide(line_in[direction, spot, piece])
                ).astype(total.dtype)

        sum_ref[:, pl.ds(piece * chunk, chunk)] = total[spot, piece]
    for far in range(chips - 1, -1, -1):
        for piece in range(RETURN_CHUNKS):
            for way in (1, -1) if far else (1,):
                block = spot + way * far

                @pl.when((block >= 0) & (block < chips))
                def _():
                    if far:
                        line_copy(block, piece, way).wait_send()
                    if pair == 2:
                        side_copy(block, piece).wait_send()


def gather_sum(parts):
    count, height, chunk = parts[0].shape
    pieces = len(parts)
    kind = parts[0].dtype
    held = pieces * parts[0].size * kind.itemsize
    pair = 2 if count % 2 == 0 else 1
    chips = count // pair
    return pl.pallas_call(
        gather_sum_kernel,
        out_shape=jax.ShapeDtypeStruct((height, pieces * chunk), kind),
        in_specs=[pl.BlockSpec(memory_space=pltpu.VMEM)] * pieces,
        out_specs=pl.BlockSpec(memory_space=pltpu.VMEM),
        scratch_shapes=[
            pltpu.VMEM((chips, pieces, height, chunk), kind),
            pltpu.VMEM((chips, pieces, height, chunk), kind),
            pltpu.VMEM((2, chips, pieces, height, chunk), kind),
            pltpu.SemaphoreType.DMA((chips, pieces)),
            pltpu.SemaphoreType.DMA((chips, pieces)),
            pltpu.SemaphoreType.DMA((chips, pieces)),
            pltpu.SemaphoreType.DMA((2, chips, pieces)),
        ],
        compiler_params=pltpu.CompilerParams(
            collective_id=1, has_side_effects=True, vmem_limit_bytes=4 * held
        ),
        cost_estimate=pl.CostEstimate(flops=0, bytes_accessed=32 * held, transcendentals=0),
    )(*[part.reshape(chips, pair, height, chunk) for part in parts])


def shifted(value, axis, steps):
    count = lax.axis_size(axis)
    initial, last = (max(0, -steps), min(count, count - steps))
    return lax.ppermute(value, axis, [(source, source + steps) for source in range(initial, last)])


def row_norm(values, gain_row):
    return (
        values * lax.rsqrt(jnp.mean(values * values, axis=-1, keepdims=True) + epsilon) * gain_row
    )


def attend(q_lat, cache_rows, new_rows, length, score_scale):
    piece_list = q_lat.shape[0]
    context = cache_rows.shape[0]
    key_rows = jnp.concatenate([cache_rows, new_rows], axis=0)
    scores = (
        jnp.einsum("thl,kl->thk", q_lat, key_rows, preferred_element_type=jnp.float32) * score_scale
    )
    position = lax.broadcasted_iota(jnp.int32, (piece_list, context + piece_list), 1)
    query_pos = lax.broadcasted_iota(jnp.int32, (piece_list, context + piece_list), 0)
    visible = jnp.where(position < context, position < length, position - context <= query_pos)
    scores = jnp.where(visible[:, None, :], scores, -jnp.inf)
    row_max = jnp.max(scores, axis=-1, keepdims=True)
    expd = jnp.where(visible[:, None, :], jnp.exp(scores - row_max), 0.0)
    attention = (expd / jnp.sum(expd, axis=-1, keepdims=True)).astype(jnp.bfloat16)
    return jnp.einsum(
        "thk,kl->thl", attention, key_rows, preferred_element_type=jnp.float32
    ).astype(jnp.bfloat16)


def shards(
    opening_residual,
    incoming_residual,
    stored_summaries,
    stored_counts,
    picked_specialists,
    chooser_mixing_share,
    mixing_scale_factor,
    asking_projection,
    summary_lookup_factor,
    summary_content_factor,
    merging_projection,
    compress_projection,
    summary_scale_factor,
    specialist_scale_factor,
    specialist_switch_factor,
    specialist_widen_factor,
    specialist_contract_factor,
):
    segment_ordinal = lax.axis_index("section")
    section_count = lax.axis_size("section")
    sources = lax.axis_size("expert")
    tick_count = stored_summaries.shape[0]
    piece_list = opening_residual.shape[1]
    inner_feature_midcount = opening_residual.shape[2]
    full_width = mixing_scale_factor.shape[1]
    local_heads = summary_lookup_factor.shape[1]
    head_size = summary_lookup_factor.shape[2]
    top_count = picked_specialists.shape[3]
    expert_local = specialist_switch_factor.shape[1]
    score_scale = head_size ** (-0.5)
    expert_ids = lax.broadcasted_iota(jnp.int32, (1, 1, 1, expert_local * sources), 3)
    shares_dense = jnp.sum(
        jnp.where(
            picked_specialists[:, 0][..., None] == expert_ids,
            chooser_mixing_share[:, 0][..., None],
            0.0,
        ),
        axis=2,
    )
    shares_dense = jnp.swapaxes(shares_dense, 1, 2)
    earlier_or_same = (
        lax.broadcasted_iota(jnp.int32, (piece_list, piece_list), 0)
        <= lax.broadcasted_iota(jnp.int32, (piece_list, piece_list), 1)
    ).astype(jnp.bfloat16)
    slots = lax.broadcasted_iota(jnp.int32, (1, 1, CAP, 1), 2) + 1
    outputs = []
    present_carry = opening_residual[0]
    section_out = present_carry
    for step_index in range(tick_count):
        if step_index > 0:
            handed = shifted(section_out, "section", 1)
            present_carry = jnp.where(
                segment_ordinal == 0, incoming_residual[step_index - 1], handed
            )
        micro_index = step_index - segment_ordinal + section_count - 1
        length = lax.dynamic_index_in_dim(stored_counts[:, 0], micro_index, 0, keepdims=False)
        full_rows = lax.all_gather(present_carry, "tensor", axis=1, tiled=True)
        normed = row_norm(full_rows.astype(jnp.float32), mixing_scale_factor[0]).astype(
            jnp.bfloat16
        )
        queries = jnp.dot(normed, asking_projection[0], preferred_element_type=jnp.float32).astype(
            jnp.bfloat16
        )
        queries = queries.reshape(piece_list, local_heads, head_size)
        q_lat = jnp.einsum(
            "thd,hdl->thl", queries, summary_lookup_factor[0], preferred_element_type=jnp.float32
        ).astype(jnp.bfloat16)
        latent_part = jnp.dot(normed, compress_projection[0], preferred_element_type=jnp.float32)
        latent_raw = lax.all_gather(
            latent_part.astype(jnp.bfloat16), "tensor", axis=1, tiled=True
        ).astype(latent_part.dtype)
        new_latent = row_norm(latent_raw, summary_scale_factor[0]).astype(jnp.bfloat16)
        o_lat = attend(q_lat, stored_summaries[step_index, 0, 0], new_latent, length, score_scale)
        heads_out = jnp.einsum(
            "thl,hld->thd", o_lat, summary_content_factor[0], preferred_element_type=jnp.float32
        ).astype(jnp.bfloat16)
        heads_out = heads_out.reshape(piece_list, local_heads * head_size)
        head_terms = jnp.dot(heads_out, merging_projection[0], preferred_element_type=jnp.float32)
        residual = present_carry.astype(jnp.float32) + lax.psum_scatter(
            head_terms.astype(jnp.bfloat16), "tensor", scatter_dimension=1, tiled=True
        ).astype(jnp.float32)
        squares = lax.psum(jnp.sum(residual * residual, axis=1), "tensor")
        moe_input = (
            residual
            * lax.rsqrt(squares / full_width + epsilon)[:, None]
            * specialist_scale_factor[0]
        ).astype(jnp.bfloat16)
        whole_rows = lax.all_gather(moe_input, "tensor", axis=1, tiled=True)
        all_rows, all_shares = spread(whole_rows, shares_dense[step_index])
        mine = lax.dynamic_slice_in_dim(
            all_shares, lax.axis_index("expert") * expert_local, expert_local, axis=1
        )
        chosen = mine > 0.0
        rank = jnp.einsum(
            "jer,rq->jeq",
            chosen.astype(jnp.bfloat16),
            earlier_or_same,
            preferred_element_type=jnp.float32,
        ).astype(jnp.int32)
        at_slot = (rank[..., None, :] == slots) & chosen[..., None, :]
        place = at_slot.astype(jnp.bfloat16)
        share = jnp.sum(jnp.where(at_slot, mine[..., None, :], 0.0), axis=-1)
        hidden_list = []
        for e in range(expert_local):
            rows_in = jnp.einsum(
                "jsr,jrd->jsd", place[:, e], all_rows, preferred_element_type=jnp.float32
            ).astype(jnp.bfloat16)
            rows_in = rows_in.reshape(sources * CAP, full_width)
            gate_values = jnp.dot(
                rows_in, specialist_switch_factor[0, e], preferred_element_type=jnp.float32
            )
            up_values = jnp.dot(
                rows_in, specialist_widen_factor[0, e], preferred_element_type=jnp.float32
            )
            hidden_list.append(
                (jax.nn.silu(gate_values) * up_values * share[:, e].reshape(-1, 1)).astype(
                    jnp.bfloat16
                )
            )
        chunk = full_width // RETURN_CHUNKS
        routed_list = []
        for c in range(RETURN_CHUNKS):
            total = None
            for e in range(expert_local):
                down = jnp.dot(
                    hidden_list[e],
                    specialist_contract_factor[0, e][:, c * chunk : (c + 1) * chunk],
                    preferred_element_type=jnp.float32,
                ).astype(jnp.bfloat16)
                term = jnp.einsum(
                    "jsr,jsd->jrd",
                    place[:, e],
                    down.reshape(sources, CAP, chunk),
                    preferred_element_type=jnp.float32,
                )
                total = term if total is None else total + term
            routed_list.append(total.astype(jnp.bfloat16))
        routed = gather_sum(routed_list)
        routed = lax.psum_scatter(routed, "tensor", scatter_dimension=1, tiled=True).astype(
            jnp.float32
        )
        section_out = (residual + routed).astype(jnp.bfloat16)
        outputs.append(section_out)
    return jnp.stack(outputs)[:, None]


def solution(mesh):
    in_specs = (
        P("section", ("groups", "expert"), "tensor"),
        P(None, ("groups", "expert"), "tensor"),
        P(None, "section", ("groups", "expert"), None, None),
        P(None, ("groups", "expert")),
        P(None, "section", ("groups", "expert"), None),
        P(None, "section", ("groups", "expert"), None),
        P("section", None),
        P("section", None, "tensor"),
        P("section", "tensor", None, None),
        P("section", "tensor", None, None),
        P("section", "tensor", None),
        P("section", None, "tensor"),
        P("section", None),
        P("section", "tensor"),
        P("section", "expert", None, "tensor"),
        P("section", "expert", None, "tensor"),
        P("section", "expert", "tensor", None),
    )
    out_specs = P(None, "section", ("groups", "expert"), "tensor")
    return jax.shard_map(shards, mesh=mesh, in_specs=in_specs, out_specs=out_specs, check_vma=False)
```
